512 devices in a mesh: layer: 8 (over z_hi, y), feat: 64 (over x, z_lo, core).
Axes of the slice: x: 4, y: 4, z: 16 (z_hi: 2, z_lo: 8; z = z_hi * 8 + z_lo), core: 2. Of those that a mesh axis runs over, the one named last changes fastest.
Arguments:
- residual: bfloat16 [8, 256, 4096], P('layer', 'feat'), may hold values from -6 to 6
- targets: bfloat16 [8, 256, 4096], P('layer', 'feat'), may hold values from -6 to 6
- w_enc: bfloat16 [8, 4096, 8192], P('layer', None, 'feat'), may hold values from -0.09375 to 0.09375
- b_enc: float32 [8, 8192], P('layer', 'feat'), may hold values from -3 to 3
- w_dec: bfloat16 [8, 8192, 4096], P('layer', 'feat'), may hold values from -0.0625 to 0.0625
- block_mask: int32 [8, 2, 64], P('layer', None, 'feat'), may hold values from 0 to 1, as said below
Outputs:
- grad_encoder: bfloat16 [8, 4096, 8192], P('layer', None, 'feat')
- grad_bias: float32 [8, 8192], P('layer', 'feat')
- grad_decoder: bfloat16 [8, 8192, 4096], P('layer', 'feat')
- loss: float32 [], replicated
The draws below stay inside these ranges and needn't reach their ends.
Inputs may be any that keep to these rules, and one draw needn't show every extreme that they name: `block_mask`: each feature block of a layer has its own activity level, so the number of active blocks differs from device to device; some feature blocks are never active and some always.
All inputs are finite; a program needn't handle non-finite values.
Results may differ from the reference program's by a relative error of at most 0.0056.
Values may be sent and summed in bfloat16 or wider, within the bound.
A program may use at most 64 MiB of HBM per device.

```python
import jax
import jax.numpy as jnp
from jax import lax

D = 4096
F = 8192
TOKENS = 256
TBLOCK = 128
FBLOCK = 128
LAYERS = 8


def draw_block_mask(key, part):
    level_key, roll_key = jax.random.split(key)
    levels = jax.random.randint(level_key, (LAYERS, 1, F // FBLOCK), 0, 5)
    rolls = jax.random.randint(roll_key, (LAYERS, TOKENS // TBLOCK, F // FBLOCK), 0, 4)
    return (rolls < levels).astype(jnp.int32)


def level_of(own_key, extent, shards, low, high):
    level = 1.0
    for axis_at, shards_of in shards:
        draws = jax.random.uniform(jax.random.fold_in(jax.random.fold_in(own_key, 6), axis_at), (shards_of,), jnp.float32, low / len(shards), high / len(shards))
        level = level * jnp.repeat(jnp.exp(draws), extent[axis_at] // shards_of).reshape((-1,) + (1,) * (len(extent) - 1 - axis_at))
    return level


def gaussian(rng, shape, spread, reach, cuts=(), held_as=jnp.bfloat16):
    entries = spread * jax.random.normal(rng, shape, jnp.float32)
    if cuts:
        entries = entries * level_of(rng, shape, cuts, -0.22, 0.18)
    return jnp.clip(entries, -reach, reach).astype(held_as)


def setup_inputs(seed: int = 0) -> dict:
    key_list = jax.random.split(jax.random.key(seed), 7)
    return {
        "residual": gaussian(key_list[0], (LAYERS, TOKENS, D), 1.0, 6.0, ((0, 8), (1, 64))),
        "targets": gaussian(key_list[1], (LAYERS, TOKENS, D), 1.0, 6.0, ((0, 8), (1, 64))),
        "w_enc": gaussian(key_list[2], (LAYERS, D, F), D ** -0.5, 0.09375, ((0, 8), (2, 64))),
        "b_enc": gaussian(key_list[3], (LAYERS, F), 0.5, 3.0, ((0, 8), (1, 64)), jnp.float32),
        "w_dec": gaussian(key_list[4], (LAYERS, F, D), F ** -0.5, 0.0625, ((0, 8), (1, 64))),
        "block_mask": draw_block_mask(jax.random.fold_in(key_list[6], 71), 0),
    }


penalty_weight = 0.5
norm_epsilon = 1e-06

def expand_mask(blocks):
    return jnp.repeat(jnp.repeat(blocks, TBLOCK, axis=0), FBLOCK, axis=1).astype(jnp.float32)

def reference(residual, targets, w_enc, b_enc, w_dec, block_mask):
    layers = residual.shape[0]
    activations = []
    positives = []
    keep_masks = []
    row_norms = []
    for layer in range(layers):
        preact = jnp.dot(residual[layer], w_enc[layer], preferred_element_type=jnp.float32) + b_enc[layer]
        positive = jnp.maximum(preact, 0.0)
        keep_mask = expand_mask(block_mask[layer])
        activations.append((keep_mask * positive * positive).astype(jnp.bfloat16))
        positives.append(positive)
        keep_masks.append(keep_mask)
        row_norms.append(jnp.sqrt(lax.optimization_barrier(jnp.sum(jnp.square(w_dec[layer].astype(jnp.float32)), axis=1)) + norm_epsilon))
    misfits = []
    square_sum = jnp.zeros((), jnp.float32)
    penalty_sum = jnp.zeros((), jnp.float32)
    for target in range(layers):
        source = (target - 1) % layers
        recon = jnp.dot(activations[source], w_dec[source], preferred_element_type=jnp.float32)
        misfit = recon - targets[target].astype(jnp.float32)
        misfits.append(misfit)
        square_sum = square_sum + jnp.sum(misfit * misfit)
    enc_grads = []
    bias_grads = []
    dec_grads = []
    for layer in range(layers):
        activation = activations[layer]
        act_float = activation.astype(jnp.float32)
        penalty_sum = penalty_sum + jnp.sum(act_float * row_norms[layer][None, :])
        error_back = misfits[(layer + 1) % layers].astype(jnp.bfloat16)
        decoder = w_dec[layer]
        dec_grad = jnp.dot(activation.T, error_back, preferred_element_type=jnp.float32)
        act_sum = lax.optimization_barrier(jnp.sum(act_float, axis=0))
        dec_grad = dec_grad + penalty_weight * act_sum[:, None] * decoder.astype(jnp.float32) / row_norms[layer][:, None]
        dec_grads.append(dec_grad.astype(jnp.bfloat16))
        act_grad = jnp.dot(error_back, decoder.T, preferred_element_type=jnp.float32)
        act_grad = act_grad + penalty_weight * row_norms[layer][None, :]
        pre_grad = (act_grad * keep_masks[layer] * 2.0 * positives[layer]).astype(jnp.bfloat16)
        bias_grads.append(lax.optimization_barrier(jnp.sum(pre_grad.astype(jnp.float32), axis=0)))
        enc_grads.append(jnp.dot(residual[layer].T, pre_grad, preferred_element_type=jnp.float32).astype(jnp.bfloat16))
    loss = (0.5 * square_sum + penalty_weight * penalty_sum) / (layers * TOKENS * D)
    return (jnp.stack(enc_grads), jnp.stack(bias_grads), jnp.stack(dec_grads), loss)
```

```python
import jax
import jax.numpy as jnp
from jax import lax
from jax.experimental import pallas as pl
from jax.experimental.pallas import tpu as pltpu
from jax.sharding import PartitionSpec as P

NX, NZ, NC, NY = 4, 8, 2, 4
TOKENS, D, FD = 256, 4096, 128
SL = D // NX
CORE_ROWS = TOKENS // NC
HALF = CORE_ROWS // 2
PR = CORE_ROWS // NZ
CHUNKS = 2
CW = SL // CHUNKS
COPIES = 256

penalty_weight = 0.5
norm_epsilon = 1e-06
f32, bf16 = jnp.float32, jnp.bfloat16


def contract_last(a, b):
    return lax.dot_general(a, b, (((1,), (1,)), ((), ())), preferred_element_type=f32)


def fold(v):
    total = None
    for r in range(0, v.shape[0], 8):
        for q in range(0, v.shape[1], 128):
            tile = v[r : r + 8, q : q + 128]
            total = tile if total is None else total + tile
    return total


def kernel(
    scale,
    mask_ref, res_ref, tgt_ref, wenc_hbm, benc_ref, wdec_hbm,
    enc_out, bias_out, dec_out, loss_out,
    raw, traw, tp, tsh, tsw, tfin, g, gt, bk, wenc, wcat, act, actcat, pos2, part, own,
    opl, opr, accr, accl, inl, inr, sumb, ssum, za, zb, zc, zr, lossb, lsend, lrecv, lz, norms, actg,
    decb, encb, send, recv, local,
):
    layer = lax.axis_index("layer")
    feat = lax.axis_index("feat")
    zh, y = layer // NY, lax.rem(layer, NY)
    c = lax.rem(feat, NC)
    z = lax.rem(feat // NC, NZ)
    x = feat // (NC * NZ)
    h, zq = z // 4, lax.rem(z, 4)
    xr, xo, xl = (lax.rem(x + d, NX) for d in (1, 2, 3))

    def dev(l=layer, xx=x, zz=z, cc=c):
        return (l, (xx * NZ + zz) * NC + cc)

    zpeers = [h * 4 + lax.rem(zq + d, 4) for d in range(4)]
    zfrom = [h * 4 + lax.rem(zq + 4 - d, 4) for d in range(4)]
    zx = lax.rem(z + 4, NZ)
    zphys = zh * NZ + z

    def far(step):
        zz = lax.rem(zphys + step, 2 * NZ)
        return dev((zz // NZ) * NY + y, x, lax.rem(zz, NZ))

    up, down = far(4), far(12)
    ydn = dev(zh * NY + lax.rem(y + 3, NY))
    yup = dev(zh * NY + lax.rem(y + 1, NY))
    mate = dev(cc=1 - c)
    right, left, opp = dev(xx=xr), dev(xx=xl), dev(xx=xo)

    used = [0]
    sends = []

    class Remote:
        def __init__(self, device):
            self.i, self.device = used[0], device
            used[0] += 1

        def go(self, src, dst, keep=True):
            d = pltpu.make_async_remote_copy(
                src, dst, send.at[self.i], recv.at[self.i],
                device_id=self.device, device_id_type=pl.DeviceIdType.MESH,
            )
            d.start()
            if keep:
                sends.append(d)
            return d

        def wait(self, landed):
            pltpu.make_async_remote_copy(
                landed, landed, send.at[self.i], recv.at[self.i],
                device_id=self.device, device_id_type=pl.DeviceIdType.MESH,
            ).wait_recv()

    wrow = pl.multiple_of(c * FD, FD)
    orow = pl.multiple_of((1 - c) * FD, FD)
    load_dec = pltpu.make_async_copy(wdec_hbm.at[0], wcat.at[pl.ds(wrow, FD)], local.at[0])
    load_enc = pltpu.make_async_copy(wenc_hbm.at[0], wenc, local.at[1])
    load_dec.start()
    load_enc.start()

    barrier = pltpu.get_barrier_semaphore()
    partners = [mate, right, left, opp, *(dev(zz=q) for q in zpeers[1:]), up, down, yup, ydn]
    for p in partners:
        pl.semaphore_signal(barrier, inc=1, device_id=p, device_id_type=pl.DeviceIdType.MESH)
    pl.semaphore_wait(barrier, len(partners))

    rows_c = c * CORE_ROWS

    def slab(xx):
        return pl.ds(pl.multiple_of(xx * SL, SL), SL)

    xdevs = {1: (right, xr), 2: (opp, xo), 3: (left, xl)}

    def stage0(src, buf, sem):
        rem = {}
        for d in (2, 1, 3):
            device, xx = xdevs[d]
            rem[d] = Remote(device)
            rem[d].go(src.at[0, :, slab(xx)], buf.at[x])
        mine = pltpu.make_async_copy(src.at[0, :, slab(x)], buf.at[x], local.at[sem])
        mine.start()

        def finish():
            mine.wait()
            for d in (1, 3, 2):
                rem[d].wait(buf.at[lax.rem(x + 4 - d, NX)])
            return jnp.concatenate([buf[i].astype(f32) for i in range(NX)], axis=0).astype(bf16)

        return finish

    res_done = stage0(res_ref, raw, 2)
    tgt_done = stage0(tgt_ref, traw, 3)

    def gather(buf, k):
        def rows(first, n, xx):
            return buf.at[
                pl.ds(pl.multiple_of(first, 16), n),
                pl.ds(pl.multiple_of(xx * SL + k * CW, CW), CW),
            ]

        def piece(zz):
            return rows(rows_c + zz * PR, PR, x)

        def half(hh, xx, cc=c):
            return rows(cc * CORE_ROWS + hh * HALF, HALF, xx)

        def quarter(hh, s, xx, cc=c):
            return rows(cc * CORE_ROWS + hh * HALF + s * (HALF // 2), HALF // 2, xx)

        z1 = [None] + [Remote(dev(zz=zpeers[d])) for d in (1, 2, 3)]
        zcr = Remote(dev(zz=zx))
        z2 = [None] + [Remote(dev(zz=zpeers[d])) for d in (1, 2, 3)]
        xrt = [Remote(right) for _ in range(2)]
        xlt = [Remote(left) for _ in range(2)]
        frt = [Remote(right) for _ in range(2)]
        flt = [Remote(left) for _ in range(2)]
        mates = []

        def hand(which, at, *key):
            m = Remote(mate)
            src = which(*key, at)
            m.go(src, src)
            mates.append((m, which, key, at))

        zcr.go(piece(z), piece(z))
        for d in (2, 1, 3):
            z1[d].go(piece(z), piece(z))
        yield
        for d in (1, 2, 3):
            z1[d].wait(piece(zfrom[d]))
        xrt[0].go(half(h, x), half(h, x))
        xlt[0].go(half(h, x), half(h, x))
        hand(half, x, h)
        yield
        zcr.wait(piece(zx))
        for d in (2, 1, 3):
            z2[d].go(piece(zx), piece(zx))
        yield
        o = 1 - h
        for d in (1, 2, 3):
            z2[d].wait(piece(lax.rem(zfrom[d] + 4, NZ)))
        xrt[1].go(half(o, x), half(o, x))
        xlt[1].go(half(o, x), half(o, x))
        hand(half, x, o)
        for i, hh in enumerate((h, o)):
            yield
            xrt[i].wait(half(hh, xl))
            frt[i].go(quarter(hh, 0, xl), quarter(hh, 0, xl))
            hand(half, xl, hh)
            xlt[i].wait(half(hh, xr))
            flt[i].go(quarter(hh, 1, xr), quarter(hh, 1, xr))
            hand(half, xr, hh)
        yield
        for i, hh in enumerate((h, o)):
            frt[i].wait(quarter(hh, 0, xo))
            hand(quarter, xo, hh, 0)
            flt[i].wait(quarter(hh, 1, xo))
            hand(quarter, xo, hh, 1)
        yield
        for m, which, key, at in mates:
            m.wait(which(*key, at, 1 - c))

    load_dec.wait()
    wd = Remote(mate)
    wd.go(wcat.at[pl.ds(wrow, FD)], wcat.at[pl.ds(wrow, FD)])

    first = res_done()
    g[pl.ds(pl.multiple_of(rows_c + z * PR, PR), PR), slab(x)] = first
    gathers = [gather(g, k) for k in range(CHUNKS)]

    def step(*gens):
        for gen in gens:
            next(gen, None)

    step(*gathers)

    tp[...] = tgt_done()
    shift = Remote(ydn)
    shift.go(tp, tsh)

    sq = jnp.zeros((FD, 128), f32)
    for q in range(0, D, 512):
        w = wcat[pl.ds(wrow, FD), q : q + 512].astype(f32)
        w = w * w
        sq = sq + (w[:, :128] + w[:, 128:256]) + (w[:, 256:384] + w[:, 384:])
    norm_col = jnp.sqrt(jnp.sum(sq, axis=1, keepdims=True) + norm_epsilon)
    norms[...] = jnp.broadcast_to(norm_col, (FD, FD)).T

    step(*gathers)
    step(*gathers)

    shift.wait(tsh)
    swap1, swap2 = Remote(up), Remote(up)
    edge = y == NY - 1

    @pl.when(edge)
    def _():
        swap1.go(tsh, tsw.at[0], keep=False)

    for _ in range(3):
        step(*gathers)

    @pl.when(edge)
    def _():
        swap1.wait(tsw.at[0])
        swap2.go(tsw.at[0], tsw.at[1], keep=False)

    for _ in range(3):
        step(*gathers)

    load_enc.wait()
    pre = jnp.dot(g[...], wenc[...], preferred_element_type=f32) + benc_ref[...]
    positive = jnp.maximum(pre, 0.0)
    at = lax.broadcasted_iota(jnp.int32, (TOKENS, FD), 0)
    keep = jnp.where(
        lax.rem(at, PR) < PR // 2, mask_ref[0].astype(f32), mask_ref[1].astype(f32)
    )
    act[...] = (keep * positive * positive).astype(bf16)
    pos2[...] = keep * 2.0 * positive
    actcat[:, pl.ds(wrow, FD)] = act[pl.ds(pl.multiple_of(rows_c, FD), FD), :]
    ax = Remote(mate)
    ax.go(act.at[pl.ds(orow, FD)], actcat.at[:, pl.ds(wrow, FD)])
    act_float = act[...].astype(f32)
    norm_row = norms[0:1, :]
    lossb[0] = fold(act_float * norm_row) * penalty_weight
    wd.wait(wcat.at[pl.ds(orow, FD)])
    ax.wait(actcat.at[:, pl.ds(orow, FD)])

    def cols(xx, k):
        return pl.ds(pl.multiple_of(xx * SL + k * CW, CW), CW)

    def decode(xx, k):
        return jnp.dot(actcat[...], wcat[:, cols(xx, k)], preferred_element_type=f32)

    lo, hi = pl.ds(0, HALF), pl.ds(HALF, HALF)

    def reduce(k):
        o_r, o_l = Remote(right), Remote(left)
        d_r, d_l = Remote(right), Remote(left)
        a_r, a_l = Remote(right), Remote(left)
        part[:, cols(xo, k)] = decode(xo, k).astype(bf16)
        o_r.go(part.at[lo, cols(xo, k)], opl.at[k])
        o_l.go(part.at[hi, cols(xo, k)], opr.at[k])
        part[:, cols(xr, k)] = decode(xr, k).astype(bf16)
        d_r.go(part.at[hi, cols(xr, k)], inl.at[k, hi])
        part[:, cols(xl, k)] = decode(xl, k).astype(bf16)
        d_l.go(part.at[lo, cols(xl, k)], inr.at[k, lo])
        own[k] = decode(x, k)
        yield
        o_r.wait(opl.at[k])
        accr[k] = (part[lo, cols(xr, k)].astype(f32) + opl[k].astype(f32)).astype(bf16)
        a_r.go(accr.at[k], inl.at[k, lo])
        o_l.wait(opr.at[k])
        accl[k] = (part[hi, cols(xl, k)].astype(f32) + opr[k].astype(f32)).astype(bf16)
        a_l.go(accl.at[k], inr.at[k, hi])
        yield
        d_r.wait(inl.at[k, hi])
        d_l.wait(inr.at[k, lo])
        a_r.wait(inl.at[k, lo])
        a_l.wait(inr.at[k, hi])
        total = own[k] + inl[k].astype(f32) + inr[k].astype(f32)
        ssum[k] = total
        sumb[k] = total.astype(bf16)

        def zrows(zz):
            return pl.ds(pl.multiple_of(zz * PR, PR), PR)

        zbr = [None] + [Remote(dev(zz=zpeers[d])) for d in (1, 2, 3)]
        zar = [None] + [Remote(dev(zz=zpeers[d])) for d in (1, 2, 3)]
        zcr = Remote(dev(zz=zx))
        for d in (2, 1, 3):
            zbr[d].go(sumb.at[k, zrows(lax.rem(zpeers[d] + 4, NZ))], zb.at[k, d - 1])
        for d in (2, 1, 3):
            zar[d].go(sumb.at[k, zrows(zpeers[d])], za.at[k, d - 1])
        yield
        for d in (1, 2, 3):
            zbr[d].wait(zb.at[k, d - 1])
        relay = ssum[k, zrows(zx)]
        for d in range(3):
            relay = relay + zb[k, d].astype(f32)
        zr[k] = relay.astype(bf16)
        zcr.go(zr.at[k], zc.at[k])
        yield
        for d in (1, 2, 3):
            zar[d].wait(za.at[k, d - 1])
        recon = ssum[k, zrows(z)]
        for d in range(3):
            recon = recon + za[k, d].astype(f32)
        zcr.wait(zc.at[k])
        recon = recon + zc[k].astype(f32)
        there = pl.ds(k * CW, CW)
        misfit = recon - tfin[:, there].astype(f32)
        bk[pl.ds(pl.multiple_of(rows_c + z * PR, PR), PR), cols(x, k)] = misfit.astype(bf16)
        lossb[0] = lossb[0] + fold(misfit * misfit) * 0.5

    def whole(k):
        yield from reduce(k)
        yield from gather(bk, k)

    pipes = [whole(k) for k in range(CHUNKS)]
    step(*pipes)

    for q in range(0, D // 2, 512):
        gt[q : q + 512, :] = g[:, q : q + 512].T
    step(*pipes)
    for q in range(D // 2, D, 512):
        gt[q : q + 512, :] = g[:, q : q + 512].T
    act_t = act[...].T
    act_sum = jnp.sum(act_t.astype(f32), axis=1, keepdims=True)
    coef = penalty_weight * act_sum / norm_col
    step(*pipes)

    @pl.when(edge)
    def _():
        swap2.wait(tsw.at[1])
        tfin[...] = tsw[1]
        for r, s, dst in ((swap1, tsh, tsw.at[0]), (swap2, tsw.at[0], tsw.at[1])):
            pltpu.make_async_remote_copy(
                s, dst, send.at[r.i], recv.at[r.i],
                device_id=r.device, device_id_type=pl.DeviceIdType.MESH,
            ).wait_send()

    @pl.when(y < NY - 1)
    def _():
        tfin[...] = tsh[...]

    step(*pipes)
    step(*pipes)

    def total_loss():
        par = lax.rem(zphys // 4, 2)
        cur = lossb[0]
        stages = [
            mate,
            dev(xx=x + 1 - 2 * lax.rem(x, 2)),
            dev(xx=3 - x),
            dev(zh * NY + y + 1 - 2 * lax.rem(y, 2)),
            dev(zh * NY + 3 - y),
            None,
            far(4 + 8 * par),
            far(12 - 8 * par),
        ]
        for i, device in enumerate(stages):
            if device is None:
                lz[zq] = cur
                group = [None] + [Remote(dev(zz=zpeers[d])) for d in (1, 2, 3)]
                for d in (1, 2, 3):
                    group[d].go(lz.at[zq], lz.at[zq])
                yield
                for d in (1, 2, 3):
                    group[d].wait(lz.at[lax.rem(zq + 4 - d, 4)])
                cur = (lz[0] + lz[1]) + (lz[2] + lz[3])
            else:
                r = Remote(device)
                lsend[i] = cur
                r.go(lsend.at[i], lrecv.at[i])
                yield
                r.wait(lrecv.at[i])
                cur = cur + lrecv[i]
        loss_out[0, 0] = jnp.sum(cur) * scale

    loss_steps = total_loss()
    outs = []

    def backward(k):
        for xx in range(NX):
            at = xx * SL + k * CW
            back = bk[:, at : at + CW]
            w = wcat[pl.ds(wrow, FD), at : at + CW]
            grad = jnp.dot(act_t, back, preferred_element_type=f32)
            decb[:, at : at + CW] = (grad + coef * w.astype(f32)).astype(bf16)
            more = contract_last(back, w)
            if k == 0 and xx == 0:
                actg[...] = more
            else:
                actg[...] += more
            out = pltpu.make_async_copy(
                decb.at[:, pl.ds(at, CW)], dec_out.at[0, :, pl.ds(at, CW)],
                local.at[4 + k * NX + xx],
            )
            out.start()
            outs.append(out)

    for _ in range(6):
        step(*pipes)
        step(loss_steps)
    for k in range(CHUNKS):
        step(pipes[k])
        backward(k)
        step(loss_steps)

    pre_grad = ((actg[...] + penalty_weight * norm_row) * pos2[...]).astype(bf16)
    bias_out[...] = jnp.sum(pre_grad.astype(f32), axis=0, keepdims=True)
    for q in range(0, D, 512):
        grad = jnp.dot(gt[q : q + 512, :], pre_grad, preferred_element_type=f32)
        encb[q : q + 512, :] = grad.astype(bf16)
        out = pltpu.make_async_copy(
            encb.at[pl.ds(q, 512)], enc_out.at[0, pl.ds(q, 512)],
            local.at[4 + CHUNKS * NX + q // 512],
        )
        out.start()
        outs.append(out)
    for _ in range(10):
        step(loss_steps)
    for gen in (*gathers, *pipes, loss_steps):
        assert next(gen, "end") == "end"
    for d in sends:
        d.wait_send()
    for out in outs:
        out.wait()
    assert used[0] <= COPIES


def body(residual, targets, w_enc, b_enc, w_dec, block_mask):
    scale = 1.0 / (lax.axis_size("layer") * TOKENS * D)
    hbm = pl.BlockSpec(memory_space=pl.ANY)
    vmem = pl.BlockSpec(memory_space=pltpu.VMEM)
    smem = pl.BlockSpec(memory_space=pltpu.SMEM)
    enc_grad, bias_grad, dec_grad, loss = pl.pallas_call(
        lambda *refs: kernel(scale, *refs),
        name="transcoder_step",
        out_shape=(
            jax.ShapeDtypeStruct((1, D, FD), bf16),
            jax.ShapeDtypeStruct((1, FD), f32),
            jax.ShapeDtypeStruct((1, FD, D), bf16),
            jax.ShapeDtypeStruct((1, 1), f32),
        ),
        in_specs=[smem, hbm, hbm, hbm, vmem, hbm],
        out_specs=(hbm, vmem, hbm, smem),
        scratch_shapes=[
            pltpu.VMEM((NX, 4, SL), bf16),
            pltpu.VMEM((NX, 4, SL), bf16),
            pltpu.VMEM((PR, SL), bf16),
            pltpu.VMEM((PR, SL), bf16),
            pltpu.VMEM((2, PR, SL), bf16),
            pltpu.VMEM((PR, SL), bf16),
            pltpu.VMEM((TOKENS, D), bf16),
            pltpu.VMEM((D, TOKENS), bf16),
            pltpu.VMEM((TOKENS, D), bf16),
            pltpu.VMEM((D, FD), bf16),
            pltpu.VMEM((NC * FD, D), bf16),
            pltpu.VMEM((TOKENS, FD), bf16),
            pltpu.VMEM((CORE_ROWS, NC * FD), bf16),
            pltpu.VMEM((TOKENS, FD), f32),
            pltpu.VMEM((CORE_ROWS, D), bf16),
            pltpu.VMEM((CHUNKS, CORE_ROWS, CW), f32),
            pltpu.VMEM((CHUNKS, HALF, CW), bf16),
            pltpu.VMEM((CHUNKS, HALF, CW), bf16),
            pltpu.VMEM((CHUNKS, HALF, CW), bf16),
            pltpu.VMEM((CHUNKS, HALF, CW), bf16),
            pltpu.VMEM((CHUNKS, CORE_ROWS, CW), bf16),
            pltpu.VMEM((CHUNKS, CORE_ROWS, CW), bf16),
            pltpu.VMEM((CHUNKS, CORE_ROWS, CW), bf16),
            pltpu.VMEM((CHUNKS, CORE_ROWS, CW), f32),
            pltpu.VMEM((CHUNKS, 3, PR, CW), bf16),
            pltpu.VMEM((CHUNKS, 3, PR, CW), bf16),
            pltpu.VMEM((CHUNKS, PR, CW), bf16),
            pltpu.VMEM((CHUNKS, PR, CW), bf16),
            pltpu.VMEM((1, 8, 128), f32),
            pltpu.VMEM((8, 8, 128), f32),
            pltpu.VMEM((8, 8, 128), f32),
            pltpu.VMEM((4, 8, 128), f32),
            pltpu.VMEM((FD, FD), f32),
            pltpu.VMEM((TOKENS, FD), f32),
            pltpu.VMEM((FD, D), bf16),
            pltpu.VMEM((D, FD), bf16),
            pltpu.SemaphoreType.DMA((COPIES,)),
            pltpu.SemaphoreType.DMA((COPIES,)),
            pltpu.SemaphoreType.DMA((32,)),
        ],
        compiler_params=pltpu.CompilerParams(
            collective_id=0, has_side_effects=True, vmem_limit_bytes=48 << 20
        ),
    )(block_mask.reshape(2), residual, targets, w_enc, b_enc, w_dec)
    return enc_grad, bias_grad, dec_grad, loss.reshape(())


def solution(mesh):
    return jax.shard_map(
        body,
        mesh=mesh,
        in_specs=(
            P("layer", "feat", None),
            P("layer", "feat", None),
            P("layer", None, "feat"),
            P("layer", "feat"),
            P("layer", "feat", None),
            P("layer", None, "feat"),
        ),
        out_specs=(P("layer", None, "feat"), P("layer", "feat"), P("layer", "feat", None), P()),
        check_vma=False,
    )
```

```python
import jax
import jax.numpy as jnp
from jax import lax
from jax.experimental import pallas as pl
from jax.experimental.pallas import tpu as pltpu
from jax.sharding import PartitionSpec as P

NX, NZ, NC, NY = 4, 8, 2, 4
TOKENS, D, FD = 256, 4096, 128
SL = D // NX
CORE_ROWS = TOKENS // NC
HALF = CORE_ROWS // 2
PR = CORE_ROWS // NZ
GCHUNKS = 2
GW = SL // GCHUNKS
CHUNKS = 2
CW = SL // CHUNKS
GROUPS = 55

penalty_weight = 0.5
norm_epsilon = 1e-06
f32, bf16 = jnp.float32, jnp.bfloat16


def contract_last(a, b):
    return lax.dot_general(a, b, (((1,), (1,)), ((), ())), preferred_element_type=f32)


def fold(v):
    total = None
    for r in range(0, v.shape[0], 8):
        for q in range(0, v.shape[1], 128):
            tile = v[r : r + 8, q : q + 128]
            total = tile if total is None else total + tile
    return total


def kernel(
    scale,
    mask_hbm, res_ref, tgt_ref, wenc_hbm, benc_hbm, wdec_hbm,
    enc_out, bias_out, dec_out, loss_out,
    mask, benc, raw, traw, tp, tsh, tsw, tfin, g, gt, bk, wenc, wcat, act, actcat, pos2,
    part, own, opl, opr, accr, accl, inl, inr, sumb, ssum, zab, zs, zc, lossb, lxc, lfar,
    lz, ly, norms, actg, send, recv, local,
):
    layer = lax.axis_index("layer")
    feat = lax.axis_index("feat")
    zh, y = layer // NY, lax.rem(layer, NY)
    c = lax.rem(feat, NC)
    z = lax.rem(feat // NC, NZ)
    x = feat // (NC * NZ)
    h, zq = z // 4, lax.rem(z, 4)
    xr, xo, xl = (lax.rem(x + d, NX) for d in (1, 2, 3))

    def dev(l=layer, xx=x, zz=z, cc=c):
        return (l, (xx * NZ + zz) * NC + cc)

    zpeers = [h * 4 + lax.rem(zq + d, 4) for d in range(4)]
    zfrom = [h * 4 + lax.rem(zq + 4 - d, 4) for d in range(4)]
    zx = lax.rem(z + 4, NZ)
    zphys = zh * NZ + z

    def far(step):
        zz = lax.rem(zphys + step, 2 * NZ)
        return dev((zz // NZ) * NY + y, x, lax.rem(zz, NZ))

    up, down = far(4), far(12)
    ys = [dev(zh * NY + lax.rem(y + d, NY)) for d in range(NY)]
    mate = dev(cc=1 - c)
    right, left, opp = dev(xx=xr), dev(xx=xl), dev(xx=xo)
    cross = dev(zz=zx)

    used = [0]
    sends = []

    class Group:
        def __init__(self, like, final=True):
            self.i, self.like = used[0], like
            used[0] += 1
            if final:
                sends.append(self)

        def copy(self, src, dst, device):
            return pltpu.make_async_remote_copy(
                src, dst, send.at[self.i], recv.at[self.i],
                device_id=device, device_id_type=pl.DeviceIdType.MESH,
            )

        def go(self, device, src, dst=None):
            self.copy(src, src if dst is None else dst, device).start()

        def wait(self):
            self.copy(self.like, self.like, mate).wait_recv()

        def sent(self):
            self.copy(self.like, self.like, mate).wait_send()

    wrow = pl.multiple_of(c * FD, FD)
    orow = pl.multiple_of((1 - c) * FD, FD)
    loads = [
        pltpu.make_async_copy(src, dst, local.at[i])
        for i, (src, dst) in enumerate((
            (wdec_hbm.at[0], wcat.at[pl.ds(wrow, FD)]), (wenc_hbm.at[0], wenc),
            (mask_hbm, mask), (benc_hbm, benc),
        ))
    ]
    for load in loads:
        load.start()

    barrier = pltpu.get_barrier_semaphore()
    partners = [
        mate, right, left, opp, *(dev(zz=q) for q in zpeers[1:]), up, down, *ys[1:],
        *(dev(xx=lax.rem(x + d, NX), cc=1 - c) for d in (1, 2, 3)),
    ]
    for p in partners:
        pl.semaphore_signal(barrier, inc=1, device_id=p, device_id_type=pl.DeviceIdType.MESH)
    pl.semaphore_wait(barrier, len(partners))

    rows_c = c * CORE_ROWS

    def slab(xx):
        return pl.ds(pl.multiple_of(xx * SL, SL), SL)

    def stage0(src, buf, sem):
        got = Group(buf.at[pl.ds(0, 3)])
        for device, xx in ((opp, xo), (right, xr), (left, xl)):
            got.go(device, src.at[0, :, slab(xx)], buf.at[x])
        mine = pltpu.make_async_copy(src.at[0, :, slab(x)], buf.at[x], local.at[sem])
        mine.start()

        def finish():
            mine.wait()
            got.wait()
            return jnp.concatenate([buf[i].astype(f32) for i in range(NX)], axis=0).astype(bf16)

        return finish

    res_done = stage0(res_ref, raw, 4)
    tgt_done = stage0(tgt_ref, traw, 5)

    def blocks(buf, k, cw):
        def rows(first, n, xx, at=0, width=cw):
            return buf.at[
                pl.ds(pl.multiple_of(first, 16), n),
                pl.ds(pl.multiple_of(xx * SL + k * cw + at, 128), width),
            ]

        return rows

    def gather(buf, k, cw):
        rows = blocks(buf, k, cw)

        def like(n, width=cw):
            return buf.at[pl.ds(0, n), pl.ds(0, width)]

        def piece(zz):
            return rows(rows_c + zz * PR, PR, x)

        def half(hh, xx):
            return rows(rows_c + hh * HALF, HALF, xx)

        def side(hh, s, xx):
            return rows(rows_c + hh * HALF, HALF, xx, s * (cw // 2), cw // 2)

        z1, zcr, z2 = Group(like(3 * PR)), Group(like(PR)), Group(like(3 * PR))
        xrt = [Group(like(HALF)) for _ in range(2)]
        xlt = [Group(like(HALF)) for _ in range(2)]
        fwd = [Group(like(HALF)) for _ in range(2)]
        mates = Group(like(CORE_ROWS, NX * cw))
        o = 1 - h

        def ring(i, zz):
            xrt[i].go(right, piece(zz))
            xlt[i].go(left, piece(zz))

        zcr.go(cross, piece(z))
        for d in (2, 1, 3):
            z1.go(dev(zz=zpeers[d]), piece(z))
        ring(0, z)
        yield
        z1.wait()
        for d in (1, 3, 2):
            ring(0, zfrom[d])
        mates.go(mate, half(h, x))
        yield
        zcr.wait()
        for d in (2, 1, 3):
            z2.go(dev(zz=zpeers[d]), piece(zx))
        ring(1, zx)
        yield
        z2.wait()
        for d in (1, 3, 2):
            ring(1, lax.rem(zfrom[d] + 4, NZ))
        mates.go(mate, half(o, x))
        for i, hh in enumerate((h, o)):
            yield
            xrt[i].wait()
            fwd[i].go(right, side(hh, 0, xl))
            mates.go(mate, half(hh, xl))
            xlt[i].wait()
            fwd[i].go(left, side(hh, 1, xr))
            mates.go(mate, half(hh, xr))
        yield
        for i, hh in enumerate((h, o)):
            fwd[i].wait()
            mates.go(mate, half(hh, xo))
        yield
        mates.wait()

    def gather2(buf, k, cw):
        rows = blocks(buf, k, cw)

        def like(n, width=cw):
            return buf.at[pl.ds(0, n), pl.ds(0, width)]

        def piece(zz):
            return rows(rows_c + zz * PR, PR, x)

        def all_of(xx, at=0, width=cw):
            return rows(rows_c, CORE_ROWS, xx, at, width)

        z1 = Group(like(6 * PR))
        xrt, xlt = Group(like(CORE_ROWS)), Group(like(CORE_ROWS))
        fwd = Group(like(CORE_ROWS))
        mates = Group(like(CORE_ROWS, NX * cw))

        def ring(zz):
            xrt.go(right, piece(zz))
            xlt.go(left, piece(zz))

        both = (zq, zq + 4)
        for d in (2, 1, 3):
            for zz in both:
                z1.go(dev(zz=zpeers[d]), piece(zz))
        for zz in both:
            ring(zz)
        yield
        z1.wait()
        for d in (1, 3, 2):
            for zz in (lax.rem(zfrom[d], 4), lax.rem(zfrom[d], 4) + 4):
                ring(zz)
        mates.go(mate, all_of(x))
        yield
        xrt.wait()
        fwd.go(right, all_of(xl, 0, cw // 2))
        xlt.wait()
        fwd.go(left, all_of(xr, cw // 2, cw // 2))
        mates.go(mate, all_of(xl))
        mates.go(mate, all_of(xr))
        yield
        fwd.wait()
        mates.go(mate, all_of(xo))
        yield
        mates.wait()

    loads[0].wait()
    wd = Group(wcat.at[pl.ds(wrow, FD)])
    wd.go(mate, wcat.at[pl.ds(wrow, FD)])

    first = res_done()
    g[pl.ds(pl.multiple_of(rows_c + z * PR, PR), PR), slab(x)] = first
    gathers = [gather(g, k, GW) for k in range(GCHUNKS)]

    def step(*gens):
        for gen in gens:
            next(gen, None)

    step(*gathers)

    tp[...] = tgt_done()
    shift = Group(tsh)
    shift.go(ys[3], tp, tsh)

    sq = jnp.zeros((FD, 128), f32)
    for q in range(0, D, 512):
        w = wcat[pl.ds(wrow, FD), q : q + 512].astype(f32)
        w = w * w
        sq = sq + (w[:, :128] + w[:, 128:256]) + (w[:, 256:384] + w[:, 384:])
    norm_col = jnp.sqrt(jnp.sum(sq, axis=1, keepdims=True) + norm_epsilon)
    norms[...] = jnp.broadcast_to(norm_col, (FD, FD)).T

    step(*gathers)
    step(*gathers)

    shift.wait()
    swap1, swap2 = Group(tsw.at[0], False), Group(tsw.at[1], False)
    edge = y == NY - 1

    @pl.when(edge)
    def _():
        swap1.go(up, tsh, tsw.at[0])

    for _ in range(3):
        step(*gathers)

    @pl.when(edge)
    def _():
        swap1.wait()
        swap2.go(up, tsw.at[0], tsw.at[1])

    for _ in range(2):
        step(*gathers)

    loads[1].wait()
    loads[2].wait()
    loads[3].wait()
    pre = jnp.dot(g[...], wenc[...], preferred_element_type=f32) + benc[...]
    positive = jnp.maximum(pre, 0.0)
    at = lax.broadcasted_iota(jnp.int32, (TOKENS, FD), 0)
    keep = jnp.where(lax.rem(at, PR) < PR // 2, mask[0].astype(f32), mask[1].astype(f32))
    act[...] = (keep * positive * positive).astype(bf16)
    pos2[...] = keep * 2.0 * positive
    ax = Group(actcat.at[:, pl.ds(0, FD)])
    ax.go(mate, act.at[pl.ds(orow, FD)], actcat.at[:, pl.ds(wrow, FD)])
    actcat[:, pl.ds(wrow, FD)] = act[pl.ds(pl.multiple_of(rows_c, FD), FD), :]
    norm_row = norms[0:1, :]
    lossb[0] = fold(act[...].astype(f32) * norm_row) * penalty_weight

    @pl.when(edge)
    def _():
        swap2.wait()
        tfin[h] = tsw[1]
        swap1.sent()
        swap2.sent()

    @pl.when(y < NY - 1)
    def _():
        tfin[h] = tsh[...]

    tx = Group(tfin.at[0])
    tx.go(cross, tfin.at[h], tfin.at[h])
    wd.wait()
    ax.wait()

    def cols(xx, k):
        return pl.ds(pl.multiple_of(xx * SL + k * CW, CW), CW)

    def decode(xx, k):
        return jnp.dot(actcat[...], wcat[:, cols(xx, k)], preferred_element_type=f32)

    lo, hi = pl.ds(0, HALF), pl.ds(HALF, HALF)

    def zrows(zz):
        return pl.ds(pl.multiple_of(zz * PR, PR), PR)

    def reduce(k):
        o_r, o_l, direct, summed = (
            Group(opl.at[k]), Group(opr.at[k]), Group(inl.at[k]), Group(inl.at[k])
        )
        part[:, cols(xo, k)] = decode(xo, k).astype(bf16)
        o_r.go(right, part.at[lo, cols(xo, k)], opl.at[k])
        o_l.go(left, part.at[hi, cols(xo, k)], opr.at[k])
        part[:, cols(xr, k)] = decode(xr, k).astype(bf16)
        direct.go(right, part.at[hi, cols(xr, k)], inl.at[k, hi])
        part[:, cols(xl, k)] = decode(xl, k).astype(bf16)
        direct.go(left, part.at[lo, cols(xl, k)], inr.at[k, lo])
        own[k] = decode(x, k)
        yield
        o_r.wait()
        accr[k] = (part[lo, cols(xr, k)].astype(f32) + opl[k].astype(f32)).astype(bf16)
        summed.go(right, accr.at[k], inl.at[k, lo])
        o_l.wait()
        accl[k] = (part[hi, cols(xl, k)].astype(f32) + opr[k].astype(f32)).astype(bf16)
        summed.go(left, accl.at[k], inr.at[k, hi])
        yield
        direct.wait()
        summed.wait()
        total = own[k] + inl[k].astype(f32) + inr[k].astype(f32)
        ssum[k] = total
        sumb[k] = total.astype(bf16)
        near = Group(zab.at[k])
        for d in (2, 1, 3):
            for hh in range(2):
                near.go(
                    dev(zz=zpeers[d]),
                    sumb.at[k, zrows(lax.rem(zpeers[d], 4) + 4 * hh)],
                    zab.at[k, d - 1, hh],
                )
        yield
        near.wait()
        for hh in range(2):
            part_sum = ssum[k, zrows(zq + 4 * hh)]
            for d in range(3):
                part_sum = part_sum + zab[k, d, hh].astype(f32)
            zs[k, hh] = part_sum.astype(bf16)
        over = Group(zc.at[k])
        over.go(cross, zs.at[k], zc.at[k])
        yield
        over.wait()
        if k == 0:
            tx.wait()
        for hh in range(2):
            recon = zs[k, hh].astype(f32) + zc[k, hh].astype(f32)
            misfit = recon - tfin[hh, :, k * CW : (k + 1) * CW].astype(f32)
            bk[pl.ds(pl.multiple_of(rows_c + (zq + 4 * hh) * PR, PR), PR), cols(x, k)] = (
                misfit.astype(bf16)
            )
            mine = (h == hh).astype(f32) * 0.5
            lossb[0] = lossb[0] + fold(misfit * misfit) * mine

    def total_loss():
        par = lax.rem(zphys // 4, 2)
        xc = x * NC + c
        s1 = Group(lxc.at[pl.ds(0, 7)])
        lxc[xc] = lossb[0]
        for d in range(NX):
            for e in range(NC):
                if d or e:
                    device = dev(xx=lax.rem(x + d, NX), cc=c if not e else 1 - c)
                    s1.go(device, lxc.at[xc])
        yield
        s1.wait()
        cur = lxc[0]
        for i in range(1, NX * NC):
            cur = cur + lxc[i]
        for i, device in enumerate((far(4 + 8 * par), far(12 - 8 * par))):
            s2 = Group(lfar.at[2 * i])
            lfar[2 * i] = cur
            s2.go(device, lfar.at[2 * i], lfar.at[2 * i + 1])
            yield
            s2.wait()
            cur = cur + lfar[2 * i + 1]
        s3 = Group(lz.at[pl.ds(0, 3)])
        lz[zq] = cur
        for d in (1, 2, 3):
            s3.go(dev(zz=zpeers[d]), lz.at[zq])
        yield
        s3.wait()
        cur = (lz[0] + lz[1]) + (lz[2] + lz[3])
        s4 = Group(ly.at[pl.ds(0, 3)])
        ly[y] = cur
        for d in (1, 2, 3):
            s4.go(ys[d], ly.at[y])
        yield
        s4.wait()
        cur = (ly[0] + ly[1]) + (ly[2] + ly[3])
        loss_out[0, 0] = jnp.sum(cur) * scale

    loss_steps = total_loss()

    def whole(k):
        yield from reduce(k)
        if k == CHUNKS - 1:
            step(loss_steps)
        yield from gather2(bk, k, CW)

    pipes = [whole(k) for k in range(CHUNKS)]
    step(*pipes)

    for q in range(0, D // 2, 512):
        gt[q : q + 512, :] = g[:, q : q + 512].T
    step(*pipes)
    for q in range(D // 2, D, 512):
        gt[q : q + 512, :] = g[:, q : q + 512].T
    act_t = act[...].T
    act_sum = jnp.sum(act_t.astype(f32), axis=1, keepdims=True)
    coef = penalty_weight * act_sum / norm_col
    for _ in range(3):
        step(*pipes)

    def backward(k):
        for xx in range(NX):
            at = xx * SL + k * CW
            back = bk[:, at : at + CW]
            w = wcat[pl.ds(wrow, FD), at : at + CW]
            grad = jnp.dot(act_t, back, preferred_element_type=f32)
            dec_out[0, :, at : at + CW] = (grad + coef * w.astype(f32)).astype(bf16)
            more = contract_last(back, w)
            if k == 0 and xx == 0:
                actg[...] = more
            else:
                actg[...] += more

    step(loss_steps)
    step(*pipes)
    step(loss_steps)
    step(*pipes)
    step(*pipes)
    step(loss_steps)
    for k in range(CHUNKS):
        step(pipes[k])
        backward(k)

    pre_grad = ((actg[...] + penalty_weight * norm_row) * pos2[...]).astype(bf16)
    bias_out[...] = jnp.sum(pre_grad.astype(f32), axis=0, keepdims=True)
    for q in range(0, D, 512):
        grad = jnp.dot(gt[q : q + 512, :], pre_grad, preferred_element_type=f32)
        enc_out[0, q : q + 512, :] = grad.astype(bf16)
    step(loss_steps)
    step(loss_steps)
    for gen in (*gathers, *pipes, loss_steps):
        assert next(gen, "end") == "end"
    for group in sends:
        group.sent()
    assert used[0] == GROUPS, used[0]


def write_out(*refs):
    copies = [
        pltpu.make_async_copy(src, dst, refs[8].at[i])
        for i, (src, dst) in enumerate(zip(refs[:4], refs[4:8]))
    ]
    for copy in copies:
        copy.start()
    for copy in copies:
        copy.wait()


def body(residual, targets, w_enc, b_enc, w_dec, block_mask):
    scale = 1.0 / (lax.axis_size("layer") * TOKENS * D)
    hbm = pl.BlockSpec(memory_space=pltpu.HBM)
    vmem = pl.BlockSpec(memory_space=pltpu.VMEM)
    smem = pl.BlockSpec(memory_space=pltpu.SMEM)
    enc_grad, bias_grad, dec_grad, loss = pl.pallas_call(
        lambda *refs: kernel(scale, *refs),
        name="transcoder_step",
        out_shape=(
            jax.ShapeDtypeStruct((1, D, FD), bf16),
            jax.ShapeDtypeStruct((1, FD), f32),
            jax.ShapeDtypeStruct((1, FD, D), bf16),
            jax.ShapeDtypeStruct((1, 1), f32),
        ),
        in_specs=[hbm] * 6,
        out_specs=(vmem, vmem, vmem, smem),
        scratch_shapes=[
            pltpu.SMEM((2,), jnp.int32),
            pltpu.VMEM((1, FD), f32),
            pltpu.VMEM((NX, 4, SL), bf16),
            pltpu.VMEM((NX, 4, SL), bf16),
            pltpu.VMEM((PR, SL), bf16),
            pltpu.VMEM((PR, SL), bf16),
            pltpu.VMEM((2, PR, SL), bf16),
            pltpu.VMEM((2, PR, SL), bf16),
            pltpu.VMEM((TOKENS, D), bf16),
            pltpu.VMEM((D, TOKENS), bf16),
            pltpu.VMEM((TOKENS, D), bf16),
            pltpu.VMEM((D, FD), bf16),
            pltpu.VMEM((NC * FD, D), bf16),
            pltpu.VMEM((TOKENS, FD), bf16),
            pltpu.VMEM((CORE_ROWS, NC * FD), bf16),
            pltpu.VMEM((TOKENS, FD), f32),
            pltpu.VMEM((CORE_ROWS, D), bf16),
            pltpu.VMEM((CHUNKS, CORE_ROWS, CW), f32),
            pltpu.VMEM((CHUNKS, HALF, CW), bf16),
            pltpu.VMEM((CHUNKS, HALF, CW), bf16),
            pltpu.VMEM((CHUNKS, HALF, CW), bf16),
            pltpu.VMEM((CHUNKS, HALF, CW), bf16),
            pltpu.VMEM((CHUNKS, CORE_ROWS, CW), bf16),
            pltpu.VMEM((CHUNKS, CORE_ROWS, CW), bf16),
            pltpu.VMEM((CHUNKS, CORE_ROWS, CW), bf16),
            pltpu.VMEM((CHUNKS, CORE_ROWS, CW), f32),
            pltpu.VMEM((CHUNKS, 3, 2, PR, CW), bf16),
            pltpu.VMEM((CHUNKS, 2, PR, CW), bf16),
            pltpu.VMEM((CHUNKS, 2, PR, CW), bf16),
            pltpu.VMEM((1, 8, 128), f32),
            pltpu.VMEM((NX * NC, 8, 128), f32),
            pltpu.VMEM((4, 8, 128), f32),
            pltpu.VMEM((4, 8, 128), f32),
            pltpu.VMEM((NY, 8, 128), f32),
            pltpu.VMEM((FD, FD), f32),
            pltpu.VMEM((TOKENS, FD), f32),
            pltpu.SemaphoreType.DMA((GROUPS,)),
            pltpu.SemaphoreType.DMA((GROUPS,)),
            pltpu.SemaphoreType.DMA((6,)),
        ],
        compiler_params=pltpu.CompilerParams(
            collective_id=0, has_side_effects=True, vmem_limit_bytes=48 << 20
        ),
    )(*(pltpu.with_memory_space_constraint(a, pltpu.HBM) for a in (block_mask.reshape(2), residual, targets, w_enc, b_enc, w_dec)))
    results = (enc_grad, bias_grad, dec_grad, loss)
    enc_grad, bias_grad, dec_grad, loss = pl.pallas_call(
        write_out,
        name="write_out",
        out_shape=tuple(jax.ShapeDtypeStruct(r.shape, r.dtype) for r in results),
        in_specs=[pl.BlockSpec(memory_space=pl.ANY)] * 4,
        out_specs=(hbm,) * 4,
        scratch_shapes=[pltpu.SemaphoreType.DMA((4,))],
        compiler_params=pltpu.CompilerParams(vmem_limit_bytes=16 << 20),
    )(*results)
    return enc_grad, bias_grad, dec_grad, loss.reshape(())


def solution(mesh):
    return jax.shard_map(
        body,
        mesh=mesh,
        in_specs=(
            P("layer", "feat", None),
            P("layer", "feat", None),
            P("layer", None, "feat"),
            P("layer", "feat"),
            P("layer", "feat", None),
            P("layer", None, "feat"),
        ),
        out_specs=(P("layer", None, "feat"), P("layer", "feat"), P("layer", "feat", None), P()),
        check_vma=False,
    )
```

```python
import math

import jax
import jax.numpy as jnp
from jax import lax
from jax.experimental import pallas as pl
from jax.experimental.pallas import tpu as pltpu
from jax.sharding import PartitionSpec as P

NX, NZ, NC, NY = 4, 8, 2, 4
TOKENS, D, FD = 256, 4096, 128
SL = D // NX
CORE_ROWS = TOKENS // NC
HALF = CORE_ROWS // 2
PR = CORE_ROWS // NZ
GCHUNKS = 2
GW = SL // GCHUNKS
CHUNKS = 2
CW = SL // CHUNKS
GROUPS = 86
POOLS = 11
SPLIT = 1
POOL = 1 << 20

penalty_weight = 0.5
norm_epsilon = 1e-06
f32, bf16 = jnp.float32, jnp.bfloat16


def contract_last(a, b):
    return lax.dot_general(a, b, (((1,), (1,)), ((), ())), preferred_element_type=f32)


def fold(v):
    total = None
    for r in range(0, v.shape[0], 8):
        for q in range(0, v.shape[1], 128):
            tile = v[r : r + 8, q : q + 128]
            total = tile if total is None else total + tile
    return total


def kernel(
    scale,
    mask_hbm, res_ref, tgt_ref, wenc_hbm, benc_hbm, wdec_hbm,
    enc_out, bias_out, dec_out, loss_out,
    mask, bcat, mk, resv, tgtv, raw, traw, tp, tsh, tsw, tfin, g, gt, bk, wencc, wcat, act, actcat,
    pos2, p2cat, part, own, opl, opr, accr, accl, inl, inr, sumb, ssum, za, zs, zc, lossb, lxc, lfar,
    lz, ly, norms, actg, send, recv, local,
):
    layer = lax.axis_index("layer")
    feat = lax.axis_index("feat")
    zh, y = layer // NY, lax.rem(layer, NY)
    c = lax.rem(feat, NC)
    z = lax.rem(feat // NC, NZ)
    x = feat // (NC * NZ)
    h, zq = z // 4, lax.rem(z, 4)
    xr, xo, xl = (lax.rem(x + d, NX) for d in (1, 2, 3))

    def dev(l=layer, xx=x, zz=z, cc=c):
        return (l, (xx * NZ + zz) * NC + cc)

    near_q = [zq + 1 - 2 * lax.rem(zq, 2), lax.rem(zq + 2, 4), 3 - zq]
    near_z = [h * 4 + q for q in near_q]
    near_dev = [dev(zz=zz) for zz in near_z]
    zx = lax.rem(z + 4, NZ)
    zphys = zh * NZ + z

    def far(step):
        zz = lax.rem(zphys + step, 2 * NZ)
        return dev((zz // NZ) * NY + y, x, lax.rem(zz, NZ))

    up, down = far(4), far(12)
    ys = [dev(zh * NY + lax.rem(y + d, NY)) for d in range(NY)]
    mate = dev(cc=1 - c)
    right, left, opp = dev(xx=xr), dev(xx=xl), dev(xx=xo)
    cross = dev(zz=zx)

    used = [0]
    pools = []

    class Group:
        def __init__(self, like, kind="main"):
            self.i, self.like = used[0], like
            used[0] += 1
            size = math.prod(like.shape) * jnp.dtype(like.dtype).itemsize
            for p, (other, total) in enumerate(pools):
                if other == kind and total + size <= POOL:
                    self.pool = p
                    pools[p] = (kind, total + size)
                    break
            else:
                self.pool = len(pools)
                pools.append((kind, size))

        def copy(self, src, dst, device):
            return pltpu.make_async_remote_copy(
                src, dst, send.at[self.pool], recv.at[self.i],
                device_id=device, device_id_type=pl.DeviceIdType.MESH,
            )

        def go(self, device, src, dst=None):
            self.copy(src, src if dst is None else dst, device).start()

        def wait(self):
            self.copy(self.like, self.like, mate).wait_recv()

    def sent(kinds):
        for p, (kind, total) in enumerate(pools):
            if kind in kinds:
                if total % 8192 == 0:
                    like = gt.at[pl.ds(0, total // 512), :]
                elif total % 4096 == 0:
                    like = gt.at[pl.ds(0, total // 256), pl.ds(0, 128)]
                else:
                    like = bcat.at[:, pl.ds(0, total // 4)]
                pltpu.make_async_remote_copy(
                    like, like, send.at[p], recv.at[0],
                    device_id=mate, device_id_type=pl.DeviceIdType.MESH,
                ).wait_send()

    wrow = pl.multiple_of(c * FD, FD)
    orow = pl.multiple_of((1 - c) * FD, FD)
    loads = [
        pltpu.make_async_copy(src, dst, local.at[i])
        for i, (src, dst) in enumerate((
            (wdec_hbm.at[0], wcat.at[pl.ds(wrow, FD)]),
            (wenc_hbm.at[0], wencc.at[:, pl.ds(wrow, FD)]),
            (mask_hbm, mask), (benc_hbm, bcat.at[:, pl.ds(wrow, FD)]),
            (res_ref, resv), (tgt_ref, tgtv),
        ))
    ]
    for load in (loads[4], loads[5], *loads[:4]):
        load.start()

    barrier = pltpu.get_barrier_semaphore()
    partners = [
        mate, right, left, opp, *near_dev, up, down, *ys[1:],
        *(dev(xx=lax.rem(x + d, NX), cc=1 - c) for d in (1, 2, 3)),
    ]
    for p in partners:
        pl.semaphore_signal(barrier, inc=1, device_id=p, device_id_type=pl.DeviceIdType.MESH)
    pl.semaphore_wait(barrier, len(partners))

    rows_c = c * CORE_ROWS

    def slab(xx):
        return pl.ds(pl.multiple_of(xx * SL, SL), SL)

    def stage0(src, buf, sem):
        got = Group(buf.at[pl.ds(0, 3)])
        for device, xx in ((opp, xo), (right, xr), (left, xl)):
            got.go(device, src.at[0, :, slab(xx)], buf.at[x])
        mine = pltpu.make_async_copy(src.at[0, :, slab(x)], buf.at[x], local.at[sem])
        mine.start()

        def finish():
            mine.wait()
            got.wait()
            return jnp.concatenate([buf[i].astype(f32) for i in range(NX)], axis=0).astype(bf16)

        return finish

    loads[4].wait()
    res_done = stage0(resv, raw, 6)
    loads[5].wait()
    tgt_done = stage0(tgtv, traw, 7)

    def blocks(buf, k, cw):
        def rows(first, n, xx, at=0, width=cw):
            return buf.at[
                pl.ds(pl.multiple_of(first, 16), n),
                pl.ds(pl.multiple_of(xx * SL + k * cw + at, 128), width),
            ]

        return rows

    def gather(buf, k, cw):
        rows = blocks(buf, k, cw)

        def like(n, width=cw):
            return buf.at[pl.ds(0, n), pl.ds(0, width)]

        def piece(zz):
            return rows(rows_c + zz * PR, PR, x)

        def side(hh, s, xx):
            return rows(rows_c + hh * HALF, HALF, xx, s * (cw // 2), cw // 2)

        zcr = Group(like(PR))
        z1 = [Group(like(PR)) for _ in range(3)]
        z2 = [Group(like(PR)) for _ in range(3)]
        xrt = [Group(like(HALF)) for _ in range(2)]
        xlt = [Group(like(HALF)) for _ in range(2)]
        fwd = [Group(like(HALF)) for _ in range(2)]
        o = 1 - h

        def ring(i, zz):
            xrt[i].go(right, piece(zz))
            xlt[i].go(left, piece(zz))

        def forward(i, hh):
            xrt[i].wait()
            fwd[i].go(right, side(hh, 0, xl))
            xlt[i].wait()
            fwd[i].go(left, side(hh, 1, xr))

        zcr.go(cross, piece(z))
        for d in range(3):
            z1[d].go(near_dev[d], piece(z))
        ring(0, z)
        for d in range(3):
            yield
            z1[d].wait()
            ring(0, near_z[d])
        yield
        zcr.wait()
        for d in (2, 1, 0):
            z2[d].go(near_dev[d], piece(zx))
        ring(1, zx)
        yield
        forward(0, h)
        for d in range(3):
            yield
            z2[d].wait()
            ring(1, lax.rem(near_z[d] + 4, NZ))
        yield
        forward(1, o)
        yield
        fwd[0].wait()
        yield
        fwd[1].wait()

    def gather2(buf, k, cw, hh):
        rows = blocks(buf, k, cw)

        def like(n, width=cw):
            return buf.at[pl.ds(0, n), pl.ds(0, width)]

        def piece(q):
            return rows(rows_c + hh * HALF + q * PR, PR, x)

        def all_of(xx, at=0, width=cw):
            return rows(rows_c + hh * HALF, HALF, xx, at, width)

        z1 = [Group(like(PR)) for _ in range(3)]
        xrt, xlt = Group(like(HALF)), Group(like(HALF))
        fwd = Group(like(HALF))
        mates = Group(like(HALF, NX * cw))

        def ring(q):
            xrt.go(right, piece(q))
            xlt.go(left, piece(q))

        for d in range(3):
            z1[d].go(near_dev[d], piece(zq))
        ring(zq)
        for d in range(3):
            yield
            z1[d].wait()
            ring(near_q[d])
        mates.go(mate, all_of(x))
        yield
        xrt.wait()
        fwd.go(right, all_of(xl, 0, cw // 2))
        xlt.wait()
        fwd.go(left, all_of(xr, cw // 2, cw // 2))
        mates.go(mate, all_of(xl))
        mates.go(mate, all_of(xr))
        yield
        fwd.wait()
        mates.go(mate, all_of(xo))
        yield
        mates.wait()

    mine = pl.ds(wrow, FD)
    loads[2].wait()
    half_tile = lax.broadcasted_iota(jnp.int32, (PR, FD), 0) < PR // 2
    mk[:, mine] = jnp.where(half_tile, mask[0].astype(f32), mask[1].astype(f32))
    loads[1].wait()
    we = Group(wencc.at[:, mine])
    we.go(mate, wencc.at[:, mine])
    loads[3].wait()
    wb = Group(bcat.at[:, mine], "odd")
    wb.go(mate, bcat.at[:, mine])
    wm = Group(mk.at[:, mine])
    wm.go(mate, mk.at[:, mine])
    loads[0].wait()
    wd = Group(wcat.at[mine])
    wd.go(mate, wcat.at[mine])

    first = res_done()
    g[pl.ds(pl.multiple_of(rows_c + z * PR, PR), PR), slab(x)] = first
    gathers = [gather(g, k, GW) for k in range(GCHUNKS)]

    def step(*gens):
        for gen in gens:
            next(gen, None)

    step(*gathers)

    tp[...] = tgt_done()
    shift = Group(tsh)
    shift.go(ys[3], tp, tsh)

    sq = jnp.zeros((FD, 128), f32)
    for q in range(0, D, 512):
        w = wcat[pl.ds(wrow, FD), q : q + 512].astype(f32)
        w = w * w
        sq = sq + (w[:, :128] + w[:, 128:256]) + (w[:, 256:384] + w[:, 384:])
    norm_col = jnp.sqrt(jnp.sum(sq, axis=1, keepdims=True) + norm_epsilon)
    norms[...] = jnp.broadcast_to(norm_col, (FD, FD)).T

    for _ in range(4):
        step(*gathers)

    shift.wait()
    swap1, swap2 = Group(tsw.at[0], "edge"), Group(tsw.at[1], "edge")
    edge = y == NY - 1

    @pl.when(edge)
    def _():
        swap1.go(up, tsh, tsw.at[0])

    for _ in range(4):
        step(*gathers)

    @pl.when(edge)
    def _():
        swap1.wait()
        swap2.go(up, tsw.at[0], tsw.at[1])

    def encode(hh):
        at = pl.multiple_of(hh * HALF, HALF)
        gx = g[pl.ds(pl.multiple_of(rows_c + at, HALF), HALF), :]
        pre = jnp.dot(gx, wencc[...], preferred_element_type=f32) + bcat[...]
        positive = jnp.maximum(pre, 0.0).reshape(HALF // PR, PR, NC * FD)
        keep = mk[...][None]
        here = pl.ds(at, HALF)
        actcat[here, :] = (keep * positive * positive).astype(bf16).reshape(HALF, NC * FD)
        p2cat[here, :] = (keep * 2.0 * positive).reshape(HALF, NC * FD)

    QUARTER = HALF // 2
    lo, hi = pl.ds(0, QUARTER), pl.ds(QUARTER, QUARTER)

    def reduce(i, hh):
        encode(hh)
        if i == 0:
            wd.wait()
        a = actcat[pl.ds(pl.multiple_of(hh * HALF, HALF), HALF), :]

        def decode(xx):
            return jnp.dot(a, wcat[:, slab(xx)], preferred_element_type=f32)

        o_r, o_l, direct, summed = (
            Group(opl.at[i]), Group(opr.at[i]), Group(inl.at[i]), Group(inl.at[i])
        )
        part[i, :, slab(xo)] = decode(xo).astype(bf16)
        o_r.go(right, part.at[i, lo, slab(xo)], opl.at[i])
        o_l.go(left, part.at[i, hi, slab(xo)], opr.at[i])
        part[i, :, slab(xr)] = decode(xr).astype(bf16)
        direct.go(right, part.at[i, hi, slab(xr)], inl.at[i, hi])
        part[i, :, slab(xl)] = decode(xl).astype(bf16)
        direct.go(left, part.at[i, lo, slab(xl)], inr.at[i, lo])
        own[i] = decode(x)
        yield
        o_r.wait()
        accr[i] = (part[i, lo, slab(xr)].astype(f32) + opl[i].astype(f32)).astype(bf16)
        summed.go(right, accr.at[i], inl.at[i, lo])
        o_l.wait()
        accl[i] = (part[i, hi, slab(xl)].astype(f32) + opr[i].astype(f32)).astype(bf16)
        summed.go(left, accl.at[i], inr.at[i, hi])
        yield
        direct.wait()
        summed.wait()
        total = own[i] + inl[i].astype(f32) + inr[i].astype(f32)
        ssum[i] = total
        sumb[i] = total.astype(bf16)

        def zrows(q):
            return pl.ds(pl.multiple_of(q * PR, PR), PR)

        parts = over[i]
        near = [Group(za.at[i, :, :, pl.ds(0, SL // len(parts))]) for _ in parts]
        w = SL // len(parts)
        for k in range(len(parts)):
            for d in (2, 1, 0):
                near[k].go(
                    near_dev[d],
                    sumb.at[i, zrows(near_q[d]), pl.ds(k * w, w)],
                    za.at[i, d, :, pl.ds(k * w, w)],
                )
        for k in range(len(parts)):
            yield
            near[k].wait()
            there = pl.ds(k * w, w)
            half_sum = ssum[i, zrows(zq), there]
            for d in range(3):
                half_sum = half_sum + za[i, d, :, there].astype(f32)
            zs[i, :, there] = half_sum.astype(bf16)
            parts[k].go(cross, zs.at[i, :, there], zc.at[1 - i, :, there])

    over = [
        [Group(zc.at[0])],
        [Group(zc.at[0, :, pl.ds(0, CW)]) for _ in range(CHUNKS)],
    ]
    early, late = reduce(0, h), reduce(1, 1 - h)

    step(*gathers)
    step(*gathers)
    we.wait()
    wb.wait()
    wm.wait()
    step(early)
    step(*gathers)
    step(early)
    step(late)
    other = pl.ds(orow, FD)
    these = pl.ds(pl.multiple_of(rows_c, CORE_ROWS), CORE_ROWS)
    gx = Group(g.at[these])
    gx.go(mate, g.at[these])
    ax, px = Group(act.at[these]), Group(pos2.at[these])
    ax.go(mate, actcat.at[:, other], act.at[these])
    px.go(mate, p2cat.at[:, other], pos2.at[these])

    @pl.when(edge)
    def _():
        swap2.wait()
        tfin[0] = tsw[1]
        sent(("edge",))

    @pl.when(y < NY - 1)
    def _():
        tfin[0] = tsh[...]

    tx = Group(tfin.at[0])
    tx.go(cross, tfin.at[0], tfin.at[1])
    act[these, :] = actcat[:, mine]
    pos2[these, :] = p2cat[:, mine]
    norm_row = norms[0:1, :]
    step(early)
    step(late)

    def transpose(first):
        for q in range(first, first + D // 2, 512):
            gt[q : q + 512, :] = g[:, q : q + 512].T

    gx.wait()
    transpose(0)
    step(late)
    ax.wait()
    px.wait()
    transpose(D // 2)
    step(early)
    act_t = act[...].T
    act_sum = jnp.sum(act_t.astype(f32), axis=1, keepdims=True)
    coef = penalty_weight * act_sum / norm_col
    lossb[0] = fold(act[...].astype(f32) * norm_row) * penalty_weight
    def finish(i, hh, k):
        there = slice(k * CW, (k + 1) * CW)
        recon = zs[i, :, there].astype(f32) + zc[i, :, there].astype(f32)
        misfit = recon - tfin[i, :, there].astype(f32)
        bk[
            pl.ds(pl.multiple_of(rows_c + (zq + 4 * hh) * PR, PR), PR),
            pl.ds(pl.multiple_of(x * SL + k * CW, CW), CW),
        ] = misfit.astype(bf16)
        if i == 1:
            lossb[0] = lossb[0] + fold(misfit * misfit) * 0.5

    def total_loss():
        par = lax.rem(zphys // 4, 2)
        xc = x * NC + c
        s1 = Group(lxc.at[pl.ds(0, 7)], "loss")
        lxc[xc] = lossb[0]
        for d in range(NX):
            for e in range(NC):
                if d or e:
                    device = dev(xx=lax.rem(x + d, NX), cc=c if not e else 1 - c)
                    s1.go(device, lxc.at[xc])
        yield
        s1.wait()
        cur = lxc[0]
        for i in range(1, NX * NC):
            cur = cur + lxc[i]
        for i, device in enumerate((far(4 + 8 * par), far(12 - 8 * par))):
            s2 = Group(lfar.at[2 * i], "loss")
            lfar[2 * i] = cur
            s2.go(device, lfar.at[2 * i], lfar.at[2 * i + 1])
            yield
            s2.wait()
            cur = cur + lfar[2 * i + 1]
        s3 = Group(lz.at[pl.ds(0, 3)], "loss")
        lz[zq] = cur
        for d in range(3):
            s3.go(near_dev[d], lz.at[zq])
        yield
        s3.wait()
        cur = (lz[0] + lz[1]) + (lz[2] + lz[3])
        s4 = Group(ly.at[pl.ds(0, 3)], "loss")
        ly[y] = cur
        for d in (1, 2, 3):
            s4.go(ys[d], ly.at[y])
        yield
        s4.wait()
        cur = (ly[0] + ly[1]) + (ly[2] + ly[3])
        loss_out[0, 0] = jnp.sum(cur) * scale

    loss_steps = total_loss()

    far_half = [gather2(bk, k, CW, 1 - h) for k in range(CHUNKS)]
    near_half = [gather2(bk, k, CW, h) for k in range(CHUNKS)]
    for k in range(CHUNKS):
        step(late)
    tx.wait()
    over[0][0].wait()
    for k in range(CHUNKS):
        finish(1, 1 - h, k)
        if k == CHUNKS - 1:
            step(loss_steps)
        step(far_half[k])

    def backward(k):
        for xx in range(NX):
            at = xx * SL + k * CW
            back = bk[:, at : at + CW]
            w = wcat[pl.ds(wrow, FD), at : at + CW]
            grad = jnp.dot(act_t, back, preferred_element_type=f32)
            dec_out[0, :, at : at + CW] = (grad + coef * w.astype(f32)).astype(bf16)
            more = contract_last(back, w)
            if k == 0 and xx == 0:
                actg[...] = more
            else:
                actg[...] += more

    step(*far_half)
    for k in range(CHUNKS):
        over[1][k].wait()
        finish(0, h, k)
        step(near_half[k])
    step(*far_half)
    step(loss_steps)
    step(*far_half)
    step(*far_half)
    step(*near_half)
    step(*near_half)
    step(*near_half)
    step(loss_steps)
    step(*far_half)
    step(*near_half)
    step(loss_steps)
    step(*near_half)
    step(*far_half)
    step(near_half[0])
    backward(0)
    step(loss_steps)
    for k in range(1, CHUNKS):
        step(near_half[k])
        backward(k)

    pre_grad = ((actg[...] + penalty_weight * norm_row) * pos2[...]).astype(bf16)
    bias_out[...] = jnp.sum(pre_grad.astype(f32), axis=0, keepdims=True)
    for q in range(0, D, 512):
        grad = jnp.dot(gt[q : q + 512, :], pre_grad, preferred_element_type=f32)
        enc_out[0, q : q + 512, :] = grad.astype(bf16)
    step(loss_steps)
    for gen in (*gathers, early, late, *far_half, *near_half, loss_steps):
        assert next(gen, "end") == "end"
    sent(("main", "odd", "loss"))
    assert (used[0], len(pools)) == (GROUPS, POOLS), (used, pools)


def write_out(*refs):
    sems = refs[8]
    pairs = []
    for src, dst in zip(refs[:4], refs[4:8]):
        rows = src.shape[1] // SPLIT if src.ndim == 3 else 0
        if rows:
            pairs += [(src.at[:, pl.ds(i * rows, rows)], dst.at[:, pl.ds(i * rows, rows)]) for i in range(SPLIT)]
        else:
            pairs.append((src, dst))
    copies = [pltpu.make_async_copy(src, dst, sems.at[i]) for i, (src, dst) in enumerate(pairs)]
    for copy in copies:
        copy.start()
    for copy in copies:
        copy.wait()


def body(residual, targets, w_enc, b_enc, w_dec, block_mask):
    scale = 1.0 / (lax.axis_size("layer") * TOKENS * D)
    hbm = pl.BlockSpec(memory_space=pltpu.HBM)
    vmem = pl.BlockSpec(memory_space=pltpu.VMEM)
    smem = pl.BlockSpec(memory_space=pltpu.SMEM)
    enc_grad, bias_grad, dec_grad, loss = pl.pallas_call(
        lambda *refs: kernel(scale, *refs),
        name="transcoder_step",
        out_shape=(
            jax.ShapeDtypeStruct((1, D, FD), bf16),
            jax.ShapeDtypeStruct((1, FD), f32),
            jax.ShapeDtypeStruct((1, FD, D), bf16),
            jax.ShapeDtypeStruct((1, 1), f32),
        ),
        in_specs=[hbm] * 6,
        out_specs=(vmem, vmem, vmem, smem),
        scratch_shapes=[
            pltpu.SMEM((2,), jnp.int32),
            pltpu.VMEM((1, NC * FD), f32),
            pltpu.VMEM((PR, NC * FD), f32),
            pltpu.VMEM((1, 4, D), bf16),
            pltpu.VMEM((1, 4, D), bf16),
            pltpu.VMEM((NX, 4, SL), bf16),
            pltpu.VMEM((NX, 4, SL), bf16),
            pltpu.VMEM((PR, SL), bf16),
            pltpu.VMEM((PR, SL), bf16),
            pltpu.VMEM((2, PR, SL), bf16),
            pltpu.VMEM((2, PR, SL), bf16),
            pltpu.VMEM((TOKENS, D), bf16),
            pltpu.VMEM((D, TOKENS), bf16),
            pltpu.VMEM((TOKENS, D), bf16),
            pltpu.VMEM((D, NC * FD), bf16),
            pltpu.VMEM((NC * FD, D), bf16),
            pltpu.VMEM((TOKENS, FD), bf16),
            pltpu.VMEM((CORE_ROWS, NC * FD), bf16),
            pltpu.VMEM((TOKENS, FD), f32),
            pltpu.VMEM((CORE_ROWS, NC * FD), f32),
            pltpu.VMEM((2, HALF, D), bf16),
            pltpu.VMEM((2, HALF, SL), f32),
            pltpu.VMEM((2, HALF // 2, SL), bf16),
            pltpu.VMEM((2, HALF // 2, SL), bf16),
            pltpu.VMEM((2, HALF // 2, SL), bf16),
            pltpu.VMEM((2, HALF // 2, SL), bf16),
            pltpu.VMEM((2, HALF, SL), bf16),
            pltpu.VMEM((2, HALF, SL), bf16),
            pltpu.VMEM((2, HALF, SL), bf16),
            pltpu.VMEM((2, HALF, SL), f32),
            pltpu.VMEM((2, 3, PR, SL), bf16),
            pltpu.VMEM((2, PR, SL), bf16),
            pltpu.VMEM((2, PR, SL), bf16),
            pltpu.VMEM((1, 8, 128), f32),
            pltpu.VMEM((NX * NC, 8, 128), f32),
            pltpu.VMEM((4, 8, 128), f32),
            pltpu.VMEM((4, 8, 128), f32),
            pltpu.VMEM((NY, 8, 128), f32),
            pltpu.VMEM((FD, FD), f32),
            pltpu.VMEM((TOKENS, FD), f32),
            pltpu.SemaphoreType.DMA((POOLS,)),
            pltpu.SemaphoreType.DMA((GROUPS,)),
            pltpu.SemaphoreType.DMA((8,)),
        ],
        compiler_params=pltpu.CompilerParams(
            collective_id=0, has_side_effects=True, vmem_limit_bytes=48 << 20
        ),
    )(*(pltpu.with_memory_space_constraint(a, pltpu.HBM) for a in (block_mask.reshape(2), residual, targets, w_enc, b_enc, w_dec)))
    results = (enc_grad, bias_grad, dec_grad, loss)
    enc_grad, bias_grad, dec_grad, loss = pl.pallas_call(
        write_out,
        name="write_out",
        out_shape=tuple(jax.ShapeDtypeStruct(r.shape, r.dtype) for r in results),
        in_specs=[pl.BlockSpec(memory_space=pl.ANY)] * 4,
        out_specs=(hbm,) * 4,
        scratch_shapes=[pltpu.SemaphoreType.DMA((2 * SPLIT + 2,))],
        compiler_params=pltpu.CompilerParams(vmem_limit_bytes=16 << 20),
    )(*results)
    return enc_grad, bias_grad, dec_grad, loss.reshape(())


def solution(mesh):
    return jax.shard_map(
        body,
        mesh=mesh,
        in_specs=(
            P("layer", "feat", None),
            P("layer", "feat", None),
            P("layer", None, "feat"),
            P("layer", "feat"),
            P("layer", "feat", None),
            P("layer", None, "feat"),
        ),
        out_specs=(P("layer", None, "feat"), P("layer", "feat"), P("layer", "feat", None), P()),
        check_vma=False,
    )
```

```python
import math

import jax
import jax.numpy as jnp
from jax import lax
from jax.experimental import pallas as pl
from jax.experimental.pallas import tpu as pltpu
from jax.sharding import PartitionSpec as P

NX, NZ, NC, NY = 4, 8, 2, 4
TOKENS, D, FD = 256, 4096, 128
SL = D // NX
CORE_ROWS = TOKENS // NC
HALF = CORE_ROWS // 2
PR = CORE_ROWS // NZ
GCHUNKS = 1
GW = SL // GCHUNKS
CHUNKS = 2
CW = SL // CHUNKS
GROUPS = 73
POOLS = 11
SPLIT = 1
POOL = 1 << 20

penalty_weight = 0.5
norm_epsilon = 1e-06
f32, bf16 = jnp.float32, jnp.bfloat16


def contract_last(a, b):
    return lax.dot_general(a, b, (((1,), (1,)), ((), ())), preferred_element_type=f32)


def fold(v):
    total = None
    for r in range(0, v.shape[0], 8):
        for q in range(0, v.shape[1], 128):
            tile = v[r : r + 8, q : q + 128]
            total = tile if total is None else total + tile
    return total


def kernel(
    scale,
    mask_hbm, res_ref, tgt_ref, wenc_hbm, benc_hbm, wdec_hbm,
    enc_out, bias_out, dec_out, loss_out,
    mask, bcat, mk, resv, tgtv, raw, traw, tp, tsh, tsw, tfin, g, gt, bk, wencc, wcat, act, actcat,
    pos2, p2cat, part, own, opl, opr, accr, accl, inl, inr, sumb, ssum, za, zs, zc, lossb, lxc, lfar,
    lz, ly, norms, actg, send, recv, local,
):
    layer = lax.axis_index("layer")
    feat = lax.axis_index("feat")
    zh, y = layer // NY, lax.rem(layer, NY)
    c = lax.rem(feat, NC)
    z = lax.rem(feat // NC, NZ)
    x = feat // (NC * NZ)
    h, zq = z // 4, lax.rem(z, 4)
    xr, xo, xl = (lax.rem(x + d, NX) for d in (1, 2, 3))

    def dev(l=layer, xx=x, zz=z, cc=c):
        return (l, (xx * NZ + zz) * NC + cc)

    near_q = [zq + 1 - 2 * lax.rem(zq, 2), lax.rem(zq + 2, 4), 3 - zq]
    near_z = [h * 4 + q for q in near_q]
    near_dev = [dev(zz=zz) for zz in near_z]
    zx = lax.rem(z + 4, NZ)
    zphys = zh * NZ + z

    def far(step):
        zz = lax.rem(zphys + step, 2 * NZ)
        return dev((zz // NZ) * NY + y, x, lax.rem(zz, NZ))

    up, down = far(4), far(12)
    ys = [dev(zh * NY + lax.rem(y + d, NY)) for d in range(NY)]
    mate = dev(cc=1 - c)
    right, left, opp = dev(xx=xr), dev(xx=xl), dev(xx=xo)
    cross = dev(zz=zx)

    used = [0]
    pools = []

    class Group:
        def __init__(self, like, kind="main"):
            self.i, self.like = used[0], like
            used[0] += 1
            size = math.prod(like.shape) * jnp.dtype(like.dtype).itemsize
            for p, (other, total) in enumerate(pools):
                if other == kind and total + size <= POOL:
                    self.pool = p
                    pools[p] = (kind, total + size)
                    break
            else:
                self.pool = len(pools)
                pools.append((kind, size))

        def copy(self, src, dst, device):
            return pltpu.make_async_remote_copy(
                src, dst, send.at[self.pool], recv.at[self.i],
                device_id=device, device_id_type=pl.DeviceIdType.MESH,
            )

        def go(self, device, src, dst=None):
            self.copy(src, src if dst is None else dst, device).start()

        def wait(self):
            self.copy(self.like, self.like, mate).wait_recv()

    def sent(kinds):
        for p, (kind, total) in enumerate(pools):
            if kind in kinds:
                if total % 8192 == 0:
                    like = gt.at[pl.ds(0, total // 512), :]
                elif total % 4096 == 0:
                    like = gt.at[pl.ds(0, total // 256), pl.ds(0, 128)]
                else:
                    like = bcat.at[:, pl.ds(0, total // 4)]
                pltpu.make_async_remote_copy(
                    like, like, send.at[p], recv.at[0],
                    device_id=mate, device_id_type=pl.DeviceIdType.MESH,
                ).wait_send()

    wrow = pl.multiple_of(c * FD, FD)
    orow = pl.multiple_of((1 - c) * FD, FD)
    loads = [
        pltpu.make_async_copy(src, dst, local.at[i])
        for i, (src, dst) in enumerate((
            (wdec_hbm.at[0], wcat.at[pl.ds(wrow, FD)]),
            (wenc_hbm.at[0], wencc.at[:, pl.ds(wrow, FD)]),
            (mask_hbm, mask), (benc_hbm, bcat.at[:, pl.ds(wrow, FD)]),
            (res_ref, resv), (tgt_ref, tgtv),
        ))
    ]
    for load in (loads[4], loads[5], *loads[:4]):
        load.start()

    barrier = pltpu.get_barrier_semaphore()
    partners = [
        mate, right, left, opp, *near_dev, up, down, *ys[1:],
        *(dev(xx=lax.rem(x + d, NX), cc=1 - c) for d in (1, 2, 3)),
    ]
    for p in partners:
        pl.semaphore_signal(barrier, inc=1, device_id=p, device_id_type=pl.DeviceIdType.MESH)
    pl.semaphore_wait(barrier, len(partners))

    rows_c = c * CORE_ROWS

    def slab(xx):
        return pl.ds(pl.multiple_of(xx * SL, SL), SL)

    def stage0(src, buf, sem):
        got = Group(buf.at[pl.ds(0, 3)])
        for device, xx in ((opp, xo), (right, xr), (left, xl)):
            got.go(device, src.at[0, :, slab(xx)], buf.at[x])
        mine = pltpu.make_async_copy(src.at[0, :, slab(x)], buf.at[x], local.at[sem])
        mine.start()

        def finish():
            mine.wait()
            got.wait()
            return jnp.concatenate([buf[i].astype(f32) for i in range(NX)], axis=0).astype(bf16)

        return finish

    loads[4].wait()
    res_done = stage0(resv, raw, 6)
    loads[5].wait()
    tgt_done = stage0(tgtv, traw, 7)

    def blocks(buf, k, cw):
        def rows(first, n, xx, at=0, width=cw):
            return buf.at[
                pl.ds(pl.multiple_of(first, 16), n),
                pl.ds(pl.multiple_of(xx * SL + k * cw + at, 128), width),
            ]

        return rows

    def gather(buf, k, cw):
        rows = blocks(buf, k, cw)

        def like(n, width=cw):
            return buf.at[pl.ds(0, n), pl.ds(0, width)]

        def piece(zz):
            return rows(rows_c + zz * PR, PR, x)

        def side(hh, s, xx):
            return rows(rows_c + hh * HALF, HALF, xx, s * (cw // 2), cw // 2)

        zcr = Group(like(PR))
        z1 = [Group(like(PR)) for _ in range(3)]
        z2 = [Group(like(PR)) for _ in range(3)]
        xrt = [Group(like(HALF)) for _ in range(2)]
        xlt = [Group(like(HALF)) for _ in range(2)]
        fwd = [Group(like(HALF)) for _ in range(2)]
        o = 1 - h

        def ring(i, zz):
            xrt[i].go(right, piece(zz))
            xlt[i].go(left, piece(zz))

        def forward(i, hh):
            xrt[i].wait()
            fwd[i].go(right, side(hh, 0, xl))
            xlt[i].wait()
            fwd[i].go(left, side(hh, 1, xr))

        zcr.go(cross, piece(z))
        for d in range(3):
            z1[d].go(near_dev[d], piece(z))
        ring(0, z)
        for d in range(3):
            yield
            z1[d].wait()
            ring(0, near_z[d])
        yield
        zcr.wait()
        for d in (2, 1, 0):
            z2[d].go(near_dev[d], piece(zx))
        ring(1, zx)
        for d in range(3):
            yield
            z2[d].wait()
            ring(1, lax.rem(near_z[d] + 4, NZ))
        yield
        forward(0, h)
        yield
        forward(1, o)
        yield
        fwd[0].wait()
        yield
        fwd[1].wait()

    def gather2(buf, k, cw, hh):
        rows = blocks(buf, k, cw)

        def like(n, width=cw):
            return buf.at[pl.ds(0, n), pl.ds(0, width)]

        def piece(q):
            return rows(rows_c + hh * HALF + q * PR, PR, x)

        def all_of(xx, at=0, width=cw):
            return rows(rows_c + hh * HALF, HALF, xx, at, width)

        z1 = [Group(like(PR)) for _ in range(3)]
        xrt, xlt = Group(like(HALF)), Group(like(HALF))
        fwd = Group(like(HALF))
        mates = Group(like(HALF, NX * cw))

        def ring(q):
            xrt.go(right, piece(q))
            xlt.go(left, piece(q))

        for d in range(3):
            z1[d].go(near_dev[d], piece(zq))
        ring(zq)
        for d in range(3):
            yield
            z1[d].wait()
            ring(near_q[d])
        mates.go(mate, all_of(x))
        yield
        xrt.wait()
        fwd.go(right, all_of(xl, 0, cw // 2))
        xlt.wait()
        fwd.go(left, all_of(xr, cw // 2, cw // 2))
        mates.go(mate, all_of(xl))
        mates.go(mate, all_of(xr))
        yield
        fwd.wait()
        mates.go(mate, all_of(xo))
        yield
        mates.wait()

    mine = pl.ds(wrow, FD)
    loads[2].wait()
    half_tile = lax.broadcasted_iota(jnp.int32, (PR, FD), 0) < PR // 2
    mk[:, mine] = jnp.where(half_tile, mask[0].astype(f32), mask[1].astype(f32))
    loads[1].wait()
    we = Group(wencc.at[:, mine])
    we.go(mate, wencc.at[:, mine])
    loads[3].wait()
    wb = Group(bcat.at[:, mine], "odd")
    wb.go(mate, bcat.at[:, mine])
    wm = Group(mk.at[:, mine])
    wm.go(mate, mk.at[:, mine])
    loads[0].wait()
    wd = Group(wcat.at[mine])
    wd.go(mate, wcat.at[mine])

    first = res_done()
    g[pl.ds(pl.multiple_of(rows_c + z * PR, PR), PR), slab(x)] = first
    gathers = [gather(g, k, GW) for k in range(GCHUNKS)]

    def step(*gens):
        for gen in gens:
            next(gen, None)

    step(*gathers)

    tp[...] = tgt_done()
    shift = Group(tsh)
    shift.go(ys[3], tp, tsh)

    sq = jnp.zeros((FD, 128), f32)
    for q in range(0, D, 512):
        w = wcat[pl.ds(wrow, FD), q : q + 512].astype(f32)
        w = w * w
        sq = sq + (w[:, :128] + w[:, 128:256]) + (w[:, 256:384] + w[:, 384:])
    norm_col = jnp.sqrt(jnp.sum(sq, axis=1, keepdims=True) + norm_epsilon)
    norms[...] = jnp.broadcast_to(norm_col, (FD, FD)).T

    for _ in range(4):
        step(*gathers)

    shift.wait()
    swap1, swap2 = Group(tsw.at[0], "edge"), Group(tsw.at[1], "edge")
    edge = y == NY - 1

    @pl.when(edge)
    def _():
        swap1.go(up, tsh, tsw.at[0])

    for _ in range(4):
        step(*gathers)

    @pl.when(edge)
    def _():
        swap1.wait()
        swap2.go(up, tsw.at[0], tsw.at[1])

    def encode(hh):
        at = pl.multiple_of(hh * HALF, HALF)
        gx = g[pl.ds(pl.multiple_of(rows_c + at, HALF), HALF), :]
        pre = jnp.dot(gx, wencc[...], preferred_element_type=f32) + bcat[...]
        positive = jnp.maximum(pre, 0.0).reshape(HALF // PR, PR, NC * FD)
        keep = mk[...][None]
        here = pl.ds(at, HALF)
        actcat[here, :] = (keep * positive * positive).astype(bf16).reshape(HALF, NC * FD)
        p2cat[here, :] = (keep * 2.0 * positive).reshape(HALF, NC * FD)

    QUARTER = HALF // 2
    lo, hi = pl.ds(0, QUARTER), pl.ds(QUARTER, QUARTER)

    def reduce(i, hh):
        encode(hh)
        if i == 0:
            wd.wait()
        a = actcat[pl.ds(pl.multiple_of(hh * HALF, HALF), HALF), :]

        def decode(xx):
            return jnp.dot(a, wcat[:, slab(xx)], preferred_element_type=f32)

        o_r, o_l, direct, summed = (
            Group(opl.at[i]), Group(opr.at[i]), Group(inl.at[i]), Group(inl.at[i])
        )

        def send_opposite():
            o_r.go(right, part.at[i, lo, slab(xo)], opl.at[i])
            o_l.go(left, part.at[i, hi, slab(xo)], opr.at[i])

        part[i, :, slab(xo)] = decode(xo).astype(bf16)
        if i == 0:
            send_opposite()
        part[i, :, slab(xr)] = decode(xr).astype(bf16)
        part[i, :, slab(xl)] = decode(xl).astype(bf16)
        own[i] = decode(x)
        if i == 1:
            yield
            send_opposite()
        direct.go(right, part.at[i, hi, slab(xr)], inl.at[i, hi])
        direct.go(left, part.at[i, lo, slab(xl)], inr.at[i, lo])
        yield
        o_r.wait()
        accr[i] = (part[i, lo, slab(xr)].astype(f32) + opl[i].astype(f32)).astype(bf16)
        summed.go(right, accr.at[i], inl.at[i, lo])
        o_l.wait()
        accl[i] = (part[i, hi, slab(xl)].astype(f32) + opr[i].astype(f32)).astype(bf16)
        summed.go(left, accl.at[i], inr.at[i, hi])
        yield
        direct.wait()
        summed.wait()
        total = own[i] + inl[i].astype(f32) + inr[i].astype(f32)
        ssum[i] = total
        sumb[i] = total.astype(bf16)

        def zrows(q):
            return pl.ds(pl.multiple_of(q * PR, PR), PR)

        parts = over[i]
        near = [Group(za.at[i, :, :, pl.ds(0, SL // len(parts))]) for _ in parts]
        w = SL // len(parts)
        for k in range(len(parts)):
            for d in (2, 1, 0):
                near[k].go(
                    near_dev[d],
                    sumb.at[i, zrows(near_q[d]), pl.ds(k * w, w)],
                    za.at[i, d, :, pl.ds(k * w, w)],
                )
        for k in range(len(parts)):
            yield
            near[k].wait()
            there = pl.ds(k * w, w)
            half_sum = ssum[i, zrows(zq), there]
            for d in range(3):
                half_sum = half_sum + za[i, d, :, there].astype(f32)
            zs[i, :, there] = half_sum.astype(bf16)
            parts[k].go(cross, zs.at[i, :, there], zc.at[1 - i, :, there])

    over = [
        [Group(zc.at[0])],
        [Group(zc.at[0, :, pl.ds(0, CW)]) for _ in range(CHUNKS)],
    ]
    early, late = reduce(0, h), reduce(1, 1 - h)

    step(*gathers)
    step(*gathers)
    we.wait()
    wb.wait()
    wm.wait()
    step(early)
    step(*gathers)
    step(late)
    step(early)
    step(late)
    other = pl.ds(orow, FD)
    these = pl.ds(pl.multiple_of(rows_c, CORE_ROWS), CORE_ROWS)
    gx = Group(g.at[these])
    gx.go(mate, g.at[these])
    ax, px = Group(act.at[these]), Group(pos2.at[these])
    ax.go(mate, actcat.at[:, other], act.at[these])
    px.go(mate, p2cat.at[:, other], pos2.at[these])

    @pl.when(edge)
    def _():
        swap2.wait()
        tfin[0] = tsw[1]
        sent(("edge",))

    @pl.when(y < NY - 1)
    def _():
        tfin[0] = tsh[...]

    tx = Group(tfin.at[0])
    tx.go(cross, tfin.at[0], tfin.at[1])
    act[these, :] = actcat[:, mine]
    pos2[these, :] = p2cat[:, mine]
    norm_row = norms[0:1, :]
    step(early)
    step(late)

    def transpose(first):
        for q in range(first, first + D // 2, 512):
            gt[q : q + 512, :] = g[:, q : q + 512].T

    gx.wait()
    transpose(0)
    step(late)
    ax.wait()
    px.wait()
    transpose(D // 2)
    step(early)
    act_t = act[...].T
    act_sum = jnp.sum(act_t.astype(f32), axis=1, keepdims=True)
    coef = penalty_weight * act_sum / norm_col
    lossb[0] = fold(act[...].astype(f32) * norm_row) * penalty_weight
    def finish(i, hh, k):
        there = slice(k * CW, (k + 1) * CW)
        recon = zs[i, :, there].astype(f32) + zc[i, :, there].astype(f32)
        misfit = recon - tfin[i, :, there].astype(f32)
        bk[
            pl.ds(pl.multiple_of(rows_c + (zq + 4 * hh) * PR, PR), PR),
            pl.ds(pl.multiple_of(x * SL + k * CW, CW), CW),
        ] = misfit.astype(bf16)
        if i == 1:
            lossb[0] = lossb[0] + fold(misfit * misfit) * 0.5

    def total_loss():
        par = lax.rem(zphys // 4, 2)
        xc = x * NC + c
        s1 = Group(lxc.at[pl.ds(0, 7)], "loss")
        lxc[xc] = lossb[0]
        for d in range(NX):
            for e in range(NC):
                if d or e:
                    device = dev(xx=lax.rem(x + d, NX), cc=c if not e else 1 - c)
                    s1.go(device, lxc.at[xc])
        yield
        s1.wait()
        cur = lxc[0]
        for i in range(1, NX * NC):
            cur = cur + lxc[i]
        for i, device in enumerate((far(4 + 8 * par), far(12 - 8 * par))):
            s2 = Group(lfar.at[2 * i], "loss")
            lfar[2 * i] = cur
            s2.go(device, lfar.at[2 * i], lfar.at[2 * i + 1])
            yield
            s2.wait()
            cur = cur + lfar[2 * i + 1]
        s3 = Group(lz.at[pl.ds(0, 3)], "loss")
        lz[zq] = cur
        for d in range(3):
            s3.go(near_dev[d], lz.at[zq])
        yield
        s3.wait()
        cur = (lz[0] + lz[1]) + (lz[2] + lz[3])
        s4 = Group(ly.at[pl.ds(0, 3)], "loss")
        ly[y] = cur
        for d in (1, 2, 3):
            s4.go(ys[d], ly.at[y])
        yield
        s4.wait()
        cur = (ly[0] + ly[1]) + (ly[2] + ly[3])
        loss_out[0, 0] = jnp.sum(cur) * scale

    loss_steps = total_loss()

    far_half = [gather2(bk, k, CW, 1 - h) for k in range(CHUNKS)]
    near_half = [gather2(bk, k, CW, h) for k in range(CHUNKS)]
    for k in range(CHUNKS):
        step(late)
    tx.wait()
    over[0][0].wait()
    for k in range(CHUNKS):
        finish(1, 1 - h, k)
        if k == CHUNKS - 1:
            step(loss_steps)
        step(far_half[k])

    def backward(k):
        for xx in range(NX):
            at = xx * SL + k * CW
            back = bk[:, at : at + CW]
            w = wcat[pl.ds(wrow, FD), at : at + CW]
            grad = jnp.dot(act_t, back, preferred_element_type=f32)
            dec_out[0, :, at : at + CW] = (grad + coef * w.astype(f32)).astype(bf16)
            more = contract_last(back, w)
            if k == 0 and xx == 0:
                actg[...] = more
            else:
                actg[...] += more

    step(*far_half)
    for k in range(CHUNKS):
        over[1][k].wait()
        finish(0, h, k)
        step(near_half[k])
    step(*far_half)
    step(loss_steps)
    step(*far_half)
    step(*far_half)
    step(*near_half)
    step(*near_half)
    step(*near_half)
    step(loss_steps)
    step(*far_half)
    step(*near_half)
    step(loss_steps)
    step(*near_half)
    step(*far_half)
    step(near_half[0])
    backward(0)
    step(loss_steps)
    for k in range(1, CHUNKS):
        step(near_half[k])
        backward(k)

    pre_grad = ((actg[...] + penalty_weight * norm_row) * pos2[...]).astype(bf16)
    bias_out[...] = jnp.sum(pre_grad.astype(f32), axis=0, keepdims=True)
    for q in range(0, D, 512):
        grad = jnp.dot(gt[q : q + 512, :], pre_grad, preferred_element_type=f32)
        enc_out[0, q : q + 512, :] = grad.astype(bf16)
    step(loss_steps)
    for gen in (*gathers, early, late, *far_half, *near_half, loss_steps):
        assert next(gen, "end") == "end"
    sent(("main", "odd", "loss"))
    assert (used[0], len(pools)) == (GROUPS, POOLS), (used, pools)


def write_out(*refs):
    sems = refs[8]
    pairs = []
    for src, dst in zip(refs[:4], refs[4:8]):
        rows = src.shape[1] // SPLIT if src.ndim == 3 else 0
        if rows:
            pairs += [(src.at[:, pl.ds(i * rows, rows)], dst.at[:, pl.ds(i * rows, rows)]) for i in range(SPLIT)]
        else:
            pairs.append((src, dst))
    copies = [pltpu.make_async_copy(src, dst, sems.at[i]) for i, (src, dst) in enumerate(pairs)]
    for copy in copies:
        copy.start()
    for copy in copies:
        copy.wait()


def body(residual, targets, w_enc, b_enc, w_dec, block_mask):
    scale = 1.0 / (lax.axis_size("layer") * TOKENS * D)
    hbm = pl.BlockSpec(memory_space=pltpu.HBM)
    vmem = pl.BlockSpec(memory_space=pltpu.VMEM)
    smem = pl.BlockSpec(memory_space=pltpu.SMEM)
    enc_grad, bias_grad, dec_grad, loss = pl.pallas_call(
        lambda *refs: kernel(scale, *refs),
        name="transcoder_step",
        out_shape=(
            jax.ShapeDtypeStruct((1, D, FD), bf16),
            jax.ShapeDtypeStruct((1, FD), f32),
            jax.ShapeDtypeStruct((1, FD, D), bf16),
            jax.ShapeDtypeStruct((1, 1), f32),
        ),
        in_specs=[hbm] * 6,
        out_specs=(vmem, vmem, vmem, smem),
        scratch_shapes=[
            pltpu.SMEM((2,), jnp.int32),
            pltpu.VMEM((1, NC * FD), f32),
            pltpu.VMEM((PR, NC * FD), f32),
            pltpu.VMEM((1, 4, D), bf16),
            pltpu.VMEM((1, 4, D), bf16),
            pltpu.VMEM((NX, 4, SL), bf16),
            pltpu.VMEM((NX, 4, SL), bf16),
            pltpu.VMEM((PR, SL), bf16),
            pltpu.VMEM((PR, SL), bf16),
            pltpu.VMEM((2, PR, SL), bf16),
            pltpu.VMEM((2, PR, SL), bf16),
            pltpu.VMEM((TOKENS, D), bf16),
            pltpu.VMEM((D, TOKENS), bf16),
            pltpu.VMEM((TOKENS, D), bf16),
            pltpu.VMEM((D, NC * FD), bf16),
            pltpu.VMEM((NC * FD, D), bf16),
            pltpu.VMEM((TOKENS, FD), bf16),
            pltpu.VMEM((CORE_ROWS, NC * FD), bf16),
            pltpu.VMEM((TOKENS, FD), f32),
            pltpu.VMEM((CORE_ROWS, NC * FD), f32),
            pltpu.VMEM((2, HALF, D), bf16),
            pltpu.VMEM((2, HALF, SL), f32),
            pltpu.VMEM((2, HALF // 2, SL), bf16),
            pltpu.VMEM((2, HALF // 2, SL), bf16),
            pltpu.VMEM((2, HALF // 2, SL), bf16),
            pltpu.VMEM((2, HALF // 2, SL), bf16),
            pltpu.VMEM((2, HALF, SL), bf16),
            pltpu.VMEM((2, HALF, SL), bf16),
            pltpu.VMEM((2, HALF, SL), bf16),
            pltpu.VMEM((2, HALF, SL), f32),
            pltpu.VMEM((2, 3, PR, SL), bf16),
            pltpu.VMEM((2, PR, SL), bf16),
            pltpu.VMEM((2, PR, SL), bf16),
            pltpu.VMEM((1, 8, 128), f32),
            pltpu.VMEM((NX * NC, 8, 128), f32),
            pltpu.VMEM((4, 8, 128), f32),
            pltpu.VMEM((4, 8, 128), f32),
            pltpu.VMEM((NY, 8, 128), f32),
            pltpu.VMEM((FD, FD), f32),
            pltpu.VMEM((TOKENS, FD), f32),
            pltpu.SemaphoreType.DMA((POOLS,)),
            pltpu.SemaphoreType.DMA((GROUPS,)),
            pltpu.SemaphoreType.DMA((8,)),
        ],
        compiler_params=pltpu.CompilerParams(
            collective_id=0, has_side_effects=True, vmem_limit_bytes=48 << 20
        ),
    )(*(pltpu.with_memory_space_constraint(a, pltpu.HBM) for a in (block_mask.reshape(2), residual, targets, w_enc, b_enc, w_dec)))
    results = (enc_grad, bias_grad, dec_grad, loss)
    enc_grad, bias_grad, dec_grad, loss = pl.pallas_call(
        write_out,
        name="write_out",
        out_shape=tuple(jax.ShapeDtypeStruct(r.shape, r.dtype) for r in results),
        in_specs=[pl.BlockSpec(memory_space=pl.ANY)] * 4,
        out_specs=(hbm,) * 4,
        scratch_shapes=[pltpu.SemaphoreType.DMA((2 * SPLIT + 2,))],
        compiler_params=pltpu.CompilerParams(vmem_limit_bytes=16 << 20),
    )(*results)
    return enc_grad, bias_grad, dec_grad, loss.reshape(())


def solution(mesh):
    return jax.shard_map(
        body,
        mesh=mesh,
        in_specs=(
            P("layer", "feat", None),
            P("layer", "feat", None),
            P("layer", None, "feat"),
            P("layer", "feat"),
            P("layer", "feat", None),
            P("layer", None, "feat"),
        ),
        out_specs=(P("layer", None, "feat"), P("layer", "feat"), P("layer", "feat", None), P()),
        check_vma=False,
    )
```

```python
import math

import jax
import jax.numpy as jnp
from jax import lax
from jax.experimental import pallas as pl
from jax.experimental.pallas import tpu as pltpu
from jax.sharding import PartitionSpec as P

NX, NZ, NC, NY = 4, 8, 2, 4
TOKENS, D, FD = 256, 4096, 128
SL = D // NX
CORE_ROWS = TOKENS // NC
HALF = CORE_ROWS // 2
PR = CORE_ROWS // NZ
GCHUNKS = 1
GW = SL // GCHUNKS
CHUNKS = 2
CW = SL // CHUNKS
GROUPS = 73
POOLS = 11
SPLIT = 1
POOL = 1 << 20

penalty_weight = 0.5
norm_epsilon = 1e-06
f32, bf16 = jnp.float32, jnp.bfloat16


def contract_last(a, b):
    return lax.dot_general(a, b, (((1,), (1,)), ((), ())), preferred_element_type=f32)


def fold(v):
    total = None
    for r in range(0, v.shape[0], 8):
        for q in range(0, v.shape[1], 128):
            tile = v[r : r + 8, q : q + 128]
            total = tile if total is None else total + tile
    return total


def kernel(
    scale,
    mask_hbm, res_ref, tgt_ref, wenc_hbm, benc_hbm, wdec_hbm,
    enc_out, bias_out, dec_out, loss_out,
    mask, bcat, mk, resv, tgtv, raw, traw, tp, tsh, tsw, tfin, g, gt, bk, wencc, wcat, act, actcat,
    pos2, p2cat, part, own, opl, opr, accr, accl, inl, inr, sumb, ssum, za, zs, zc, lossb, lxc, lfar,
    lz, ly, norms, actg, send, recv, local,
):
    layer = lax.axis_index("layer")
    feat = lax.axis_index("feat")
    zh, y = layer // NY, lax.rem(layer, NY)
    c = lax.rem(feat, NC)
    z = lax.rem(feat // NC, NZ)
    x = feat // (NC * NZ)
    h, zq = z // 4, lax.rem(z, 4)
    xr, xo, xl = (lax.rem(x + d, NX) for d in (1, 2, 3))

    def dev(l=layer, xx=x, zz=z, cc=c):
        return (l, (xx * NZ + zz) * NC + cc)

    near_q = [zq + 1 - 2 * lax.rem(zq, 2), lax.rem(zq + 2, 4), 3 - zq]
    near_z = [h * 4 + q for q in near_q]
    near_dev = [dev(zz=zz) for zz in near_z]
    zx = lax.rem(z + 4, NZ)
    zphys = zh * NZ + z

    def far(step):
        zz = lax.rem(zphys + step, 2 * NZ)
        return dev((zz // NZ) * NY + y, x, lax.rem(zz, NZ))

    up, down = far(4), far(12)
    ys = [dev(zh * NY + lax.rem(y + d, NY)) for d in range(NY)]
    mate = dev(cc=1 - c)
    right, left, opp = dev(xx=xr), dev(xx=xl), dev(xx=xo)
    cross = dev(zz=zx)

    used = [0]
    pools = []

    class Group:
        def __init__(self, like, kind="main"):
            self.i, self.like = used[0], like
            used[0] += 1
            size = math.prod(like.shape) * jnp.dtype(like.dtype).itemsize
            for p, (other, total) in enumerate(pools):
                if other == kind and total + size <= POOL:
                    self.pool = p
                    pools[p] = (kind, total + size)
                    break
            else:
                self.pool = len(pools)
                pools.append((kind, size))

        def copy(self, src, dst, device):
            return pltpu.make_async_remote_copy(
                src, dst, send.at[self.pool], recv.at[self.i],
                device_id=device, device_id_type=pl.DeviceIdType.MESH,
            )

        def go(self, device, src, dst=None):
            self.copy(src, src if dst is None else dst, device).start()

        def wait(self):
            self.copy(self.like, self.like, mate).wait_recv()

    def sent(kinds):
        for p, (kind, total) in enumerate(pools):
            if kind in kinds:
                if total % 8192 == 0:
                    like = gt.at[pl.ds(0, total // 512), :]
                elif total % 4096 == 0:
                    like = gt.at[pl.ds(0, total // 256), pl.ds(0, 128)]
                else:
                    like = bcat.at[:, pl.ds(0, total // 4)]
                pltpu.make_async_remote_copy(
                    like, like, send.at[p], recv.at[0],
                    device_id=mate, device_id_type=pl.DeviceIdType.MESH,
                ).wait_send()

    wrow = pl.multiple_of(c * FD, FD)
    orow = pl.multiple_of((1 - c) * FD, FD)
    loads = [
        pltpu.make_async_copy(src, dst, local.at[i])
        for i, (src, dst) in enumerate((
            (wdec_hbm.at[0], wcat.at[pl.ds(wrow, FD)]),
            (wenc_hbm.at[0], wencc.at[:, pl.ds(wrow, FD)]),
            (mask_hbm, mask), (benc_hbm, bcat.at[:, pl.ds(wrow, FD)]),
            (res_ref, resv), (tgt_ref, tgtv),
        ))
    ]
    for load in (loads[4], loads[5], *loads[:4]):
        load.start()

    barrier = pltpu.get_barrier_semaphore()
    partners = [
        mate, right, left, opp, *near_dev, up, down, *ys[1:],
        *(dev(xx=lax.rem(x + d, NX), cc=1 - c) for d in (1, 2, 3)),
    ]
    for p in partners:
        pl.semaphore_signal(barrier, inc=1, device_id=p, device_id_type=pl.DeviceIdType.MESH)
    pl.semaphore_wait(barrier, len(partners))

    rows_c = c * CORE_ROWS

    def slab(xx):
        return pl.ds(pl.multiple_of(xx * SL, SL), SL)

    def stage0(src, buf, sem):
        got = Group(buf.at[pl.ds(0, 3)])
        for device, xx in ((opp, xo), (right, xr), (left, xl)):
            got.go(device, src.at[0, :, slab(xx)], buf.at[x])
        mine = pltpu.make_async_copy(src.at[0, :, slab(x)], buf.at[x], local.at[sem])
        mine.start()

        def finish():
            mine.wait()
            got.wait()
            return jnp.concatenate([buf[i].astype(f32) for i in range(NX)], axis=0).astype(bf16)

        return finish

    loads[4].wait()
    res_done = stage0(resv, raw, 6)
    loads[5].wait()
    tgt_done = stage0(tgtv, traw, 7)

    def blocks(buf, k, cw):
        def rows(first, n, xx, at=0, width=cw):
            return buf.at[
                pl.ds(pl.multiple_of(first, 16), n),
                pl.ds(pl.multiple_of(xx * SL + k * cw + at, 128), width),
            ]

        return rows

    def gather(buf, k, cw):
        rows = blocks(buf, k, cw)

        def like(n, width=cw):
            return buf.at[pl.ds(0, n), pl.ds(0, width)]

        def piece(zz):
            return rows(rows_c + zz * PR, PR, x)

        def side(hh, s, xx):
            return rows(rows_c + hh * HALF, HALF, xx, s * (cw // 2), cw // 2)

        zcr = Group(like(PR))
        z1 = [Group(like(PR)) for _ in range(3)]
        z2 = [Group(like(PR)) for _ in range(3)]
        xrt = [Group(like(HALF)) for _ in range(2)]
        xlt = [Group(like(HALF)) for _ in range(2)]
        fwd = [Group(like(HALF)) for _ in range(2)]
        o = 1 - h

        def ring(i, zz):
            xrt[i].go(right, piece(zz))
            xlt[i].go(left, piece(zz))

        def forward(i, hh):
            xrt[i].wait()
            fwd[i].go(right, side(hh, 0, xl))
            xlt[i].wait()
            fwd[i].go(left, side(hh, 1, xr))

        zcr.go(cross, piece(z))
        for d in range(3):
            z1[d].go(near_dev[d], piece(z))
        ring(0, z)
        for d in range(3):
            yield
            z1[d].wait()
            ring(0, near_z[d])
        yield
        zcr.wait()
        for d in (2, 1, 0):
            z2[d].go(near_dev[d], piece(zx))
        ring(1, zx)
        for d in range(3):
            yield
            z2[d].wait()
            ring(1, lax.rem(near_z[d] + 4, NZ))
        yield
        forward(0, h)
        yield
        forward(1, o)
        yield
        fwd[0].wait()
        yield
        fwd[1].wait()

    def gather2(buf, k, cw, hh):
        rows = blocks(buf, k, cw)

        def like(n, width=cw):
            return buf.at[pl.ds(0, n), pl.ds(0, width)]

        def piece(q):
            return rows(rows_c + hh * HALF + q * PR, PR, x)

        def all_of(xx, at=0, width=cw):
            return rows(rows_c + hh * HALF, HALF, xx, at, width)

        z1 = [Group(like(PR)) for _ in range(3)]
        xrt, xlt = Group(like(HALF)), Group(like(HALF))
        fwd = Group(like(HALF))
        mates = Group(like(HALF, NX * cw))

        def ring(q):
            xrt.go(right, piece(q))
            xlt.go(left, piece(q))

        for d in range(3):
            z1[d].go(near_dev[d], piece(zq))
        ring(zq)
        for d in range(3):
            yield
            z1[d].wait()
            ring(near_q[d])
        mates.go(mate, all_of(x))
        yield
        xrt.wait()
        fwd.go(right, all_of(xl, 0, cw // 2))
        xlt.wait()
        fwd.go(left, all_of(xr, cw // 2, cw // 2))
        mates.go(mate, all_of(xl))
        mates.go(mate, all_of(xr))
        yield
        fwd.wait()
        mates.go(mate, all_of(xo))
        yield
        mates.wait()

    mine = pl.ds(wrow, FD)
    loads[2].wait()
    half_tile = lax.broadcasted_iota(jnp.int32, (PR, FD), 0) < PR // 2
    mk[:, mine] = jnp.where(half_tile, mask[0].astype(f32), mask[1].astype(f32))
    loads[1].wait()
    we = Group(wencc.at[:, mine])
    we.go(mate, wencc.at[:, mine])
    loads[3].wait()
    wb = Group(bcat.at[:, mine], "odd")
    wb.go(mate, bcat.at[:, mine])
    wm = Group(mk.at[:, mine])
    wm.go(mate, mk.at[:, mine])
    loads[0].wait()
    wd = Group(wcat.at[mine])
    wd.go(mate, wcat.at[mine])

    first = res_done()
    g[pl.ds(pl.multiple_of(rows_c + z * PR, PR), PR), slab(x)] = first
    gathers = [gather(g, k, GW) for k in range(GCHUNKS)]

    def step(*gens):
        for gen in gens:
            next(gen, None)

    step(*gathers)

    tp[...] = tgt_done()
    shift = Group(tsh)
    shift.go(ys[3], tp, tsh)

    sq = jnp.zeros((FD, 128), f32)
    for q in range(0, D, 512):
        w = wcat[pl.ds(wrow, FD), q : q + 512].astype(f32)
        w = w * w
        sq = sq + (w[:, :128] + w[:, 128:256]) + (w[:, 256:384] + w[:, 384:])
    norm_col = jnp.sqrt(jnp.sum(sq, axis=1, keepdims=True) + norm_epsilon)
    norms[...] = jnp.broadcast_to(norm_col, (FD, FD)).T

    for _ in range(4):
        step(*gathers)

    shift.wait()
    swap1, swap2 = Group(tsw.at[0], "edge"), Group(tsw.at[1], "edge")
    edge = y == NY - 1

    @pl.when(edge)
    def _():
        swap1.go(up, tsh, tsw.at[0])

    for _ in range(4):
        step(*gathers)

    @pl.when(edge)
    def _():
        swap1.wait()
        swap2.go(up, tsw.at[0], tsw.at[1])

    def encode(hh):
        at = pl.multiple_of(hh * HALF, HALF)
        gx = g[pl.ds(pl.multiple_of(rows_c + at, HALF), HALF), :]
        pre = jnp.dot(gx, wencc[...], preferred_element_type=f32) + bcat[...]
        positive = jnp.maximum(pre, 0.0).reshape(HALF // PR, PR, NC * FD)
        keep = mk[...][None]
        here = pl.ds(at, HALF)
        actcat[here, :] = (keep * positive * positive).astype(bf16).reshape(HALF, NC * FD)
        p2cat[here, :] = (keep * 2.0 * positive).reshape(HALF, NC * FD)

    QUARTER = HALF // 2
    lo, hi = pl.ds(0, QUARTER), pl.ds(QUARTER, QUARTER)

    def reduce(i, hh):
        encode(hh)
        if i == 0:
            wd.wait()
        a = actcat[pl.ds(pl.multiple_of(hh * HALF, HALF), HALF), :]

        def decode(xx):
            return jnp.dot(a, wcat[:, slab(xx)], preferred_element_type=f32)

        o_r, o_l, direct, summed = (
            Group(opl.at[i]), Group(opr.at[i]), Group(inl.at[i]), Group(inl.at[i])
        )

        def send_opposite():
            o_r.go(right, part.at[i, lo, slab(xo)], opl.at[i])
            o_l.go(left, part.at[i, hi, slab(xo)], opr.at[i])

        part[i, :, slab(xo)] = decode(xo).astype(bf16)
        if i == 0:
            send_opposite()
        part[i, :, slab(xr)] = decode(xr).astype(bf16)
        part[i, :, slab(xl)] = decode(xl).astype(bf16)
        own[i] = decode(x)
        if i == 1:
            yield
            send_opposite()
        direct.go(right, part.at[i, hi, slab(xr)], inl.at[i, hi])
        direct.go(left, part.at[i, lo, slab(xl)], inr.at[i, lo])
        yield
        o_r.wait()
        accr[i] = (part[i, lo, slab(xr)].astype(f32) + opl[i].astype(f32)).astype(bf16)
        summed.go(right, accr.at[i], inl.at[i, lo])
        o_l.wait()
        accl[i] = (part[i, hi, slab(xl)].astype(f32) + opr[i].astype(f32)).astype(bf16)
        summed.go(left, accl.at[i], inr.at[i, hi])
        yield
        direct.wait()
        summed.wait()
        total = own[i] + inl[i].astype(f32) + inr[i].astype(f32)
        ssum[i] = total
        sumb[i] = total.astype(bf16)

        def zrows(q):
            return pl.ds(pl.multiple_of(q * PR, PR), PR)

        parts = over[i]
        near = [Group(za.at[i, :, :, pl.ds(0, SL // len(parts))]) for _ in parts]
        w = SL // len(parts)
        for k in range(len(parts)):
            for d in (2, 1, 0):
                near[k].go(
                    near_dev[d],
                    sumb.at[i, zrows(near_q[d]), pl.ds(k * w, w)],
                    za.at[i, d, :, pl.ds(k * w, w)],
                )
        for k in range(len(parts)):
            yield
            near[k].wait()
            there = pl.ds(k * w, w)
            half_sum = ssum[i, zrows(zq), there]
            for d in range(3):
                half_sum = half_sum + za[i, d, :, there].astype(f32)
            zs[i, :, there] = half_sum.astype(bf16)
            parts[k].go(cross, zs.at[i, :, there], zc.at[1 - i, :, there])

    over = [
        [Group(zc.at[0])],
        [Group(zc.at[0, :, pl.ds(0, CW)]) for _ in range(CHUNKS)],
    ]
    early, late = reduce(0, h), reduce(1, 1 - h)

    step(*gathers)
    step(*gathers)
    we.wait()
    wb.wait()
    wm.wait()
    step(early)
    step(*gathers)
    step(late)
    step(early)
    step(late)
    other = pl.ds(orow, FD)
    these = pl.ds(pl.multiple_of(rows_c, CORE_ROWS), CORE_ROWS)
    gx = Group(g.at[these])
    gx.go(mate, g.at[these])
    ax, px = Group(act.at[these]), Group(pos2.at[these])
    ax.go(mate, actcat.at[:, other], act.at[these])
    px.go(mate, p2cat.at[:, other], pos2.at[these])

    @pl.when(edge)
    def _():
        swap2.wait()
        tfin[0] = tsw[1]
        sent(("edge",))

    @pl.when(y < NY - 1)
    def _():
        tfin[0] = tsh[...]

    tx = Group(tfin.at[0])
    tx.go(cross, tfin.at[0], tfin.at[1])
    act[these, :] = actcat[:, mine]
    pos2[these, :] = p2cat[:, mine]
    norm_row = norms[0:1, :]
    step(early)
    step(late)

    def transpose(first):
        for q in range(first, first + D // 2, 512):
            gt[q : q + 512, :] = g[:, q : q + 512].T

    gx.wait()
    transpose(0)
    step(early)
    step(late)
    ax.wait()
    px.wait()
    transpose(D // 2)
    act_t = act[...].T
    act_sum = jnp.sum(act_t.astype(f32), axis=1, keepdims=True)
    coef = penalty_weight * act_sum / norm_col
    lossb[0] = fold(act[...].astype(f32) * norm_row) * penalty_weight
    def finish(i, hh, k):
        there = slice(k * CW, (k + 1) * CW)
        recon = zs[i, :, there].astype(f32) + zc[i, :, there].astype(f32)
        misfit = recon - tfin[i, :, there].astype(f32)
        bk[
            pl.ds(pl.multiple_of(rows_c + (zq + 4 * hh) * PR, PR), PR),
            pl.ds(pl.multiple_of(x * SL + k * CW, CW), CW),
        ] = misfit.astype(bf16)
        if i == 1:
            lossb[0] = lossb[0] + fold(misfit * misfit) * 0.5

    def total_loss():
        par = lax.rem(zphys // 4, 2)
        xc = x * NC + c
        s1 = Group(lxc.at[pl.ds(0, 7)], "loss")
        lxc[xc] = lossb[0]
        for d in range(NX):
            for e in range(NC):
                if d or e:
                    device = dev(xx=lax.rem(x + d, NX), cc=c if not e else 1 - c)
                    s1.go(device, lxc.at[xc])
        yield
        s1.wait()
        cur = lxc[0]
        for i in range(1, NX * NC):
            cur = cur + lxc[i]
        for i, device in enumerate((far(4 + 8 * par), far(12 - 8 * par))):
            s2 = Group(lfar.at[2 * i], "loss")
            lfar[2 * i] = cur
            s2.go(device, lfar.at[2 * i], lfar.at[2 * i + 1])
            yield
            s2.wait()
            cur = cur + lfar[2 * i + 1]
        s3 = Group(lz.at[pl.ds(0, 3)], "loss")
        lz[zq] = cur
        for d in range(3):
            s3.go(near_dev[d], lz.at[zq])
        yield
        s3.wait()
        cur = (lz[0] + lz[1]) + (lz[2] + lz[3])
        s4 = Group(ly.at[pl.ds(0, 3)], "loss")
        ly[y] = cur
        for d in (1, 2, 3):
            s4.go(ys[d], ly.at[y])
        yield
        s4.wait()
        cur = (ly[0] + ly[1]) + (ly[2] + ly[3])
        loss_out[0, 0] = jnp.sum(cur) * scale

    loss_steps = total_loss()

    far_half = [gather2(bk, k, CW, 1 - h) for k in range(CHUNKS)]
    near_half = [gather2(bk, k, CW, h) for k in range(CHUNKS)]
    for k in range(CHUNKS):
        step(late)
    tx.wait()
    over[0][0].wait()
    for k in range(CHUNKS):
        finish(1, 1 - h, k)
        if k == CHUNKS - 1:
            step(loss_steps)
        step(far_half[k])

    def backward(k):
        for xx in range(NX):
            at = xx * SL + k * CW
            back = bk[:, at : at + CW]
            w = wcat[pl.ds(wrow, FD), at : at + CW]
            grad = jnp.dot(act_t, back, preferred_element_type=f32)
            dec_out[0, :, at : at + CW] = (grad + coef * w.astype(f32)).astype(bf16)
            more = contract_last(back, w)
            if k == 0 and xx == 0:
                actg[...] = more
            else:
                actg[...] += more

    step(*far_half)
    for k in range(CHUNKS):
        over[1][k].wait()
        finish(0, h, k)
        step(near_half[k])
    step(*far_half)
    step(loss_steps)
    step(*far_half)
    step(*far_half)
    step(*near_half)
    step(*near_half)
    step(*near_half)
    step(loss_steps)
    step(*far_half)
    step(*near_half)
    step(loss_steps)
    step(*near_half)
    step(*far_half)
    step(loss_steps)
    step(near_half[0])
    backward(0)
    for k in range(1, CHUNKS):
        step(near_half[k])
        backward(k)

    pre_grad = ((actg[...] + penalty_weight * norm_row) * pos2[...]).astype(bf16)
    bias_out[...] = jnp.sum(pre_grad.astype(f32), axis=0, keepdims=True)
    for q in range(0, D, 512):
        grad = jnp.dot(gt[q : q + 512, :], pre_grad, preferred_element_type=f32)
        enc_out[0, q : q + 512, :] = grad.astype(bf16)
    step(loss_steps)
    for gen in (*gathers, early, late, *far_half, *near_half, loss_steps):
        assert next(gen, "end") == "end"
    sent(("main", "odd", "loss"))
    assert (used[0], len(pools)) == (GROUPS, POOLS), (used, pools)


def write_out(*refs):
    sems = refs[8]
    pairs = []
    for src, dst in zip(refs[:4], refs[4:8]):
        rows = src.shape[1] // SPLIT if src.ndim == 3 else 0
        if rows:
            pairs += [(src.at[:, pl.ds(i * rows, rows)], dst.at[:, pl.ds(i * rows, rows)]) for i in range(SPLIT)]
        else:
            pairs.append((src, dst))
    copies = [pltpu.make_async_copy(src, dst, sems.at[i]) for i, (src, dst) in enumerate(pairs)]
    for copy in copies:
        copy.start()
    for copy in copies:
        copy.wait()


def body(residual, targets, w_enc, b_enc, w_dec, block_mask):
    scale = 1.0 / (lax.axis_size("layer") * TOKENS * D)
    hbm = pl.BlockSpec(memory_space=pltpu.HBM)
    vmem = pl.BlockSpec(memory_space=pltpu.VMEM)
    smem = pl.BlockSpec(memory_space=pltpu.SMEM)
    enc_grad, bias_grad, dec_grad, loss = pl.pallas_call(
        lambda *refs: kernel(scale, *refs),
        name="transcoder_step",
        out_shape=(
            jax.ShapeDtypeStruct((1, D, FD), bf16),
            jax.ShapeDtypeStruct((1, FD), f32),
            jax.ShapeDtypeStruct((1, FD, D), bf16),
            jax.ShapeDtypeStruct((1, 1), f32),
        ),
        in_specs=[hbm] * 6,
        out_specs=(vmem, vmem, vmem, smem),
        scratch_shapes=[
            pltpu.SMEM((2,), jnp.int32),
            pltpu.VMEM((1, NC * FD), f32),
            pltpu.VMEM((PR, NC * FD), f32),
            pltpu.VMEM((1, 4, D), bf16),
            pltpu.VMEM((1, 4, D), bf16),
            pltpu.VMEM((NX, 4, SL), bf16),
            pltpu.VMEM((NX, 4, SL), bf16),
            pltpu.VMEM((PR, SL), bf16),
            pltpu.VMEM((PR, SL), bf16),
            pltpu.VMEM((2, PR, SL), bf16),
            pltpu.VMEM((2, PR, SL), bf16),
            pltpu.VMEM((TOKENS, D), bf16),
            pltpu.VMEM((D, TOKENS), bf16),
            pltpu.VMEM((TOKENS, D), bf16),
            pltpu.VMEM((D, NC * FD), bf16),
            pltpu.VMEM((NC * FD, D), bf16),
            pltpu.VMEM((TOKENS, FD), bf16),
            pltpu.VMEM((CORE_ROWS, NC * FD), bf16),
            pltpu.VMEM((TOKENS, FD), f32),
            pltpu.VMEM((CORE_ROWS, NC * FD), f32),
            pltpu.VMEM((2, HALF, D), bf16),
            pltpu.VMEM((2, HALF, SL), f32),
            pltpu.VMEM((2, HALF // 2, SL), bf16),
            pltpu.VMEM((2, HALF // 2, SL), bf16),
            pltpu.VMEM((2, HALF // 2, SL), bf16),
            pltpu.VMEM((2, HALF // 2, SL), bf16),
            pltpu.VMEM((2, HALF, SL), bf16),
            pltpu.VMEM((2, HALF, SL), bf16),
            pltpu.VMEM((2, HALF, SL), bf16),
            pltpu.VMEM((2, HALF, SL), f32),
            pltpu.VMEM((2, 3, PR, SL), bf16),
            pltpu.VMEM((2, PR, SL), bf16),
            pltpu.VMEM((2, PR, SL), bf16),
            pltpu.VMEM((1, 8, 128), f32),
            pltpu.VMEM((NX * NC, 8, 128), f32),
            pltpu.VMEM((4, 8, 128), f32),
            pltpu.VMEM((4, 8, 128), f32),
            pltpu.VMEM((NY, 8, 128), f32),
            pltpu.VMEM((FD, FD), f32),
            pltpu.VMEM((TOKENS, FD), f32),
            pltpu.SemaphoreType.DMA((POOLS,)),
            pltpu.SemaphoreType.DMA((GROUPS,)),
            pltpu.SemaphoreType.DMA((8,)),
        ],
        compiler_params=pltpu.CompilerParams(
            collective_id=0, has_side_effects=True, vmem_limit_bytes=48 << 20
        ),
    )(*(pltpu.with_memory_space_constraint(a, pltpu.HBM) for a in (block_mask.reshape(2), residual, targets, w_enc, b_enc, w_dec)))
    results = (enc_grad, bias_grad, dec_grad, loss)
    enc_grad, bias_grad, dec_grad, loss = pl.pallas_call(
        write_out,
        name="write_out",
        out_shape=tuple(jax.ShapeDtypeStruct(r.shape, r.dtype) for r in results),
        in_specs=[pl.BlockSpec(memory_space=pl.ANY)] * 4,
        out_specs=(hbm,) * 4,
        scratch_shapes=[pltpu.SemaphoreType.DMA((2 * SPLIT + 2,))],
        compiler_params=pltpu.CompilerParams(vmem_limit_bytes=16 << 20),
    )(*results)
    return enc_grad, bias_grad, dec_grad, loss.reshape(())


def solution(mesh):
    return jax.shard_map(
        body,
        mesh=mesh,
        in_specs=(
            P("layer", "feat", None),
            P("layer", "feat", None),
            P("layer", None, "feat"),
            P("layer", "feat"),
            P("layer", "feat", None),
            P("layer", None, "feat"),
        ),
        out_specs=(P("layer", None, "feat"), P("layer", "feat"), P("layer", "feat", None), P()),
        check_vma=False,
    )
```
